1024 devices in a mesh: seq: 128 (over z, x), kvh: 8 (over y, core).
Axes of the slice: x: 4, y: 4, z: 32, core: 2. Of those that a mesh axis runs over, the one named last changes fastest.
Arguments:
- queries: bfloat16 [16384, 64, 128], P('seq', 'kvh'), may hold values from -160 to 160
- keys: bfloat16 [16384, 8, 128], P('seq', 'kvh'), may hold values from -4 to 4
- values: bfloat16 [16384, 8, 128], P('seq', 'kvh'), may hold values from -6 to 6
- output_gradient: bfloat16 [16384, 64, 128], P(('seq', 'kvh')), may hold values from -6 to 6
- doc_lengths: int32 [128], replicated, may hold values from 1 to 256, 16384 in all
- prefix_lengths: int32 [128], replicated, may hold values from 0 to 127
Outputs:
- grad_queries: bfloat16 [16384, 64, 128], P(('seq', 'kvh'))
- grad_keys: bfloat16 [16384, 8, 128], P('seq', 'kvh')
- grad_values: bfloat16 [16384, 8, 128], P('seq', 'kvh')
The draws below stay inside these ranges and needn't reach their ends.
Inputs may be any that keep to these rules, and one draw needn't show every extreme that they name: `doc_lengths`: lengths sum to 16384; the longest document has exactly 256 tokens.
All inputs are finite; a program needn't handle non-finite values.
Results may differ from the reference program's by a relative error of at most 0.015.
Values may be sent and summed in bfloat16 or wider, within the bound.
A program may use at most 32 MiB of HBM per device.

```python
import math
import jax
import jax.numpy as jnp
import numpy as np
from jax import lax

QUERY_HEADS = 64
KEY_VALUE_HEADS = 8
HEAD_DIM = 128
QUERY_PER_KV = 8
SHARD_TOKENS = 128
BACK = 2
AHEAD = 1
STREAM_TOKENS = 16384
DOCS = 128
MOST = 256
N_SEQ = 128


def paired_draw(key):
    key_sample = jnp.clip(jax.random.normal(jax.random.fold_in(key, 31), (STREAM_TOKENS, KEY_VALUE_HEADS, HEAD_DIM), jnp.float32), -4.0, 4.0)
    query_draw = jnp.clip(jax.random.normal(jax.random.fold_in(key, 32), (STREAM_TOKENS, QUERY_HEADS, HEAD_DIM), jnp.float32), -4.0, 4.0)
    return (query_draw, key_sample)


def draw_queries(key, part):
    return paired_draw(key)[0].astype(jnp.bfloat16)


def draw_keys(key, part):
    return paired_draw(key)[1].astype(jnp.bfloat16)


def draw_prefix_lengths(key, part):
    highest = AHEAD * SHARD_TOKENS
    drawn = jax.random.randint(jax.random.fold_in(key, 21), (DOCS,), 0, highest, dtype=jnp.int32)
    chosen_doc = jax.random.randint(jax.random.fold_in(key, 22), (), 0, DOCS, dtype=jnp.int32)
    doc_slots = jnp.arange(DOCS, dtype=jnp.int32)
    drawn = jnp.where(doc_slots == chosen_doc, highest - 1, drawn)
    drawn = jnp.where(doc_slots == (chosen_doc + 1) % DOCS, 0, drawn)
    return drawn.astype(jnp.int32)


def steps_of(own_key, dims, shards, low, largest):
    gain, own = 1.0, jax.random.fold_in(own_key, 6)
    for dim, parts in shards:
        heights = jnp.exp(jax.random.uniform(jax.random.fold_in(own, dim), (parts,), jnp.float32, low / len(shards), largest / len(shards)))
        gain = gain * jnp.repeat(heights, dims[dim] // parts).reshape([-1 if axis == dim else 1 for axis in range(len(dims))])
    return gain


def split_up(number_of, total, reach, slope):
    loads = [(1 << 20) // math.isqrt(rank ** slope) + 1 for rank in range(2, number_of + 1)]
    rest, holding = total - reach - (number_of - 1), [1] * (number_of - 1)
    while rest > 0:
        candidates = [i for i in range(number_of - 1) if holding[i] < reach]
        mass, budget = sum([loads[i] for i in candidates]), rest
        for i in candidates:
            addition = min(reach - holding[i], max(1, budget * loads[i] // mass), rest)
            holding[i] = holding[i] + addition
            rest = rest - addition
    return np.array([reach] + holding)


def uneven(rng, amount, total, limit, skew):
    if amount == 2:
        one = jax.random.randint(rng, (), max(1, total - limit), min(limit, total - 1) + 1)
        return jnp.stack([one, total - one])
    lengths = jnp.asarray(split_up(amount, total, limit, skew), jnp.int32)
    couples = (amount - 1) // 2
    donor, taker = lengths[1:1 + 2 * couples:2], lengths[2:2 + 2 * couples:2]
    room = jnp.minimum(donor - 1, limit - taker)
    passed = jax.random.randint(jax.random.fold_in(rng, 1), (couples,), 0, 1 << 20) % (room + 1)
    lengths = lengths.at[1:1 + 2 * couples:2].set(donor - passed).at[2:2 + 2 * couples:2].set(taker + passed)
    return lengths[jax.random.permutation(jax.random.fold_in(rng, 2), amount)]


def scatter_about(stream_key, shape, width, bound, pieces=(), kind=jnp.bfloat16):
    entries = jax.random.normal(stream_key, shape, jnp.float32) * width
    if len(pieces) > 0:
        entries = steps_of(stream_key, shape, pieces, -0.22, 0.18) * entries
    return jnp.clip(entries, min=-bound, max=bound).astype(kind)


def setup_inputs(seed: int = 0) -> dict:
    key_of = jax.random.split(jax.random.key(seed), 7)
    return {
        "queries": draw_queries(jax.random.fold_in(key_of[6], 71), 0),
        "keys": draw_keys(jax.random.fold_in(key_of[6], 71), 0),
        "values": scatter_about(key_of[2], (STREAM_TOKENS, KEY_VALUE_HEADS, HEAD_DIM), 1.0, 6.0, ((0, 128), (1, 8))),
        "output_gradient": scatter_about(key_of[3], (STREAM_TOKENS, QUERY_HEADS, HEAD_DIM), 1.0, 6.0, ((0, 1024),)),
        "doc_lengths": uneven(key_of[4], DOCS, STREAM_TOKENS, MOST, 2).astype(jnp.int32),
        "prefix_lengths": draw_prefix_lengths(jax.random.fold_in(key_of[6], 71), 0),
    }


def locate(positions, doc_end):
    return jnp.sum((positions[:, None] >= doc_end[None, :]).astype(jnp.int32), axis=1)


def reference(queries, keys, values, output_gradient, doc_lengths, prefix_lengths):
    score_scale = HEAD_DIM ** -0.5
    doc_end = jnp.cumsum(doc_lengths).astype(jnp.int32)
    prefix_end = (doc_end - doc_lengths + prefix_lengths).astype(jnp.int32)
    positions = jnp.arange(STREAM_TOKENS, dtype=jnp.int32)
    doc_index = locate(positions, doc_end)
    leading_part = BACK * SHARD_TOKENS
    trailing_part = AHEAD * SHARD_TOKENS
    window = leading_part + SHARD_TOKENS + trailing_part
    keys_padded = jnp.pad(keys, ((leading_part, trailing_part), (0, 0), (0, 0)))
    values_padded = jnp.pad(values, ((leading_part, trailing_part), (0, 0), (0, 0)))
    key_pos_all = jnp.arange(-leading_part, STREAM_TOKENS + trailing_part, dtype=jnp.int32)
    key_doc_all = jnp.pad(doc_index, (leading_part, trailing_part), constant_values=-1).astype(jnp.int32)
    key_prefix_all = jnp.where(key_doc_all >= 0, prefix_end[jnp.clip(key_doc_all, 0, DOCS - 1)], 0).astype(jnp.int32)

    def advance(accums, shard):
        keys_acc, values_acc = accums
        first_row = (shard * SHARD_TOKENS).astype(jnp.int32)
        query_tile_rows = lax.dynamic_slice_in_dim(queries, first_row, SHARD_TOKENS, 0).astype(jnp.float32).reshape(SHARD_TOKENS, KEY_VALUE_HEADS, QUERY_PER_KV, HEAD_DIM)
        cotangent_block = lax.dynamic_slice_in_dim(output_gradient, first_row, SHARD_TOKENS, 0).astype(jnp.float32).reshape(SHARD_TOKENS, KEY_VALUE_HEADS, QUERY_PER_KV, HEAD_DIM)
        key_window = lax.dynamic_slice_in_dim(keys_padded, first_row, window, 0).astype(jnp.float32)
        value_window = lax.dynamic_slice_in_dim(values_padded, first_row, window, 0).astype(jnp.float32)
        key_pos = lax.dynamic_slice_in_dim(key_pos_all, first_row, window, 0)
        key_doc = lax.dynamic_slice_in_dim(key_doc_all, first_row, window, 0)
        key_prefix = lax.dynamic_slice_in_dim(key_prefix_all, first_row, window, 0)
        query_pos = first_row + jnp.arange(SHARD_TOKENS, dtype=jnp.int32)
        query_doc = lax.dynamic_slice_in_dim(doc_index, first_row, SHARD_TOKENS, 0)
        visible = (query_doc[:, None] == key_doc[None, :]) & ((key_pos[None, :] <= query_pos[:, None]) | (key_pos[None, :] < key_prefix[None, :]))
        scores = jnp.einsum("tgqd,sgd->gqts", query_tile_rows, key_window) * score_scale
        scores = jnp.where(visible[None, None], scores, -1e30)
        row_max = jnp.max(scores, axis=-1)
        expo = jnp.where(visible[None, None], jnp.exp(scores - row_max[..., None]), 0.0)
        row_sum = jnp.sum(expo, axis=-1)
        probs = expo / row_sum[..., None]
        probs_half = probs.astype(jnp.bfloat16)
        dprobs = jnp.einsum("tgqd,sgd->gqts", cotangent_block, value_window)
        row_delta = jnp.sum(probs * dprobs, axis=-1)
        dscores = (probs * (dprobs - row_delta[..., None])).astype(jnp.bfloat16)
        dscores_wide = dscores.astype(jnp.float32)
        grad_q = (score_scale * jnp.einsum("gqts,sgd->tgqd", dscores_wide, key_window)).astype(jnp.bfloat16)
        grad_k = score_scale * jnp.einsum("gqts,tgqd->sgd", dscores_wide, query_tile_rows)
        grad_v = jnp.einsum("gqts,tgqd->sgd", probs_half.astype(jnp.float32), cotangent_block)
        keys_acc = lax.dynamic_update_slice_in_dim(keys_acc, lax.dynamic_slice_in_dim(keys_acc, first_row, window, 0) + grad_k, first_row, 0)
        values_acc = lax.dynamic_update_slice_in_dim(values_acc, lax.dynamic_slice_in_dim(values_acc, first_row, window, 0) + grad_v, first_row, 0)
        return (keys_acc, values_acc), grad_q.reshape(SHARD_TOKENS, QUERY_HEADS, HEAD_DIM)

    zero_accumulator = jnp.zeros((STREAM_TOKENS + leading_part + trailing_part, KEY_VALUE_HEADS, HEAD_DIM), jnp.float32)
    (keys_acc, values_acc), query_blocks = lax.scan(advance, (zero_accumulator, zero_accumulator), jnp.arange(N_SEQ, dtype=jnp.int32))
    grad_queries = query_blocks.reshape(STREAM_TOKENS, QUERY_HEADS, HEAD_DIM)
    grad_keys = keys_acc[leading_part:leading_part + STREAM_TOKENS].astype(jnp.bfloat16)
    grad_values = values_acc[leading_part:leading_part + STREAM_TOKENS].astype(jnp.bfloat16)
    return (grad_queries, grad_keys, grad_values)
```

```python
import functools

import jax
import jax.numpy as jnp
from jax import lax
from jax.experimental import pallas as pl
from jax.experimental.pallas import tpu as pltpu
from jax.sharding import PartitionSpec as P

MESH = pl.DeviceIdType.MESH
GROUP = 8
TILES = 4
LOG2E = 1.4426950408889634
NT = (((1,), (1,)), ((), ()))


def key_interval(positions, doc_len, doc_prefix, doc_start):
    start = jnp.max(jnp.where(doc_start <= positions, doc_start, 0), axis=0, keepdims=True)
    mine = doc_start == start
    length = jnp.sum(jnp.where(mine, doc_len, 0), axis=0, keepdims=True)
    prefix = jnp.sum(jnp.where(mine, doc_prefix, 0), axis=0, keepdims=True)
    stop = jnp.minimum(start + length, jnp.maximum(positions + 1, start + prefix))
    return start, stop


def kernel(
    n_seq, n_kvh, scale,
    q_hbm, k_hbm, v_hbm, og_hbm, len_hbm, pre_hbm,
    gq_out, gk_out, gv_out,
    qbuf, kbuf, vbuf, cot, lens, pres, q2, c2, probs, probs_half, dscores, gqbuf,
    part_out, part_in, own, final,
    local_sem, kv_send, kv_recv, cot_send, cot_recv, gq_send, gq_recv, part_send, part_recv, out_sem,
):
    seq = lax.axis_index("seq")
    me = lax.axis_index("kvh")
    chip = me // 2
    chips = n_kvh // 2
    partner = me + 1 - 2 * lax.rem(me, 2)
    rows = q2.shape[0]
    tokens = kbuf.shape[1]
    piece = rows // n_kvh
    width = 2 * piece

    def shard(distance):
        return lax.rem(seq + distance + n_seq, n_seq)

    barrier = pltpu.get_barrier_semaphore()
    others = [(seq, lax.rem(me + d, n_kvh)) for d in range(1, n_kvh)]
    others += [(shard(d), me) for d in (-2, -1, 1, 2)]
    for other in others:
        pl.semaphore_signal(barrier, inc=1, device_id=other, device_id_type=MESH)

    local = [
        pltpu.make_async_copy(len_hbm, lens, local_sem.at[0]),
        pltpu.make_async_copy(pre_hbm, pres, local_sem.at[1]),
        pltpu.make_async_copy(q_hbm, qbuf, local_sem.at[2]),
        pltpu.make_async_copy(k_hbm, kbuf.at[2], local_sem.at[3]),
        pltpu.make_async_copy(v_hbm, vbuf.at[2], local_sem.at[4]),
        pltpu.make_async_copy(og_hbm.at[:, me], cot.at[me], cot_recv.at[me]),
    ]
    for copy in local:
        copy.start()
    pl.semaphore_wait(barrier, len(others))

    sends = []
    for number, (distance, slot) in enumerate(((2, 0), (1, 1), (-1, 3))):
        copy = pltpu.make_async_remote_copy(
            k_hbm, kbuf.at[slot], kv_send.at[0, number], kv_recv.at[0, number],
            device_id=(shard(distance), me), device_id_type=MESH,
        )
        copy.start()
        sends.append(copy)
    targets = [2 * lax.rem(chip + d, chips) + core for d in (2, 1, 3) for core in (0, 1)]
    targets.append(partner)
    for number, target in enumerate(targets):
        copy = pltpu.make_async_remote_copy(
            og_hbm.at[:, target], cot.at[me], cot_send.at[number], cot_recv.at[me],
            device_id=(seq, target), device_id_type=MESH,
        )
        copy.start()
        sends.append(copy)
    for number, (distance, slot) in enumerate(((2, 0), (1, 1), (-1, 3))):
        copy = pltpu.make_async_remote_copy(
            v_hbm, vbuf.at[slot], kv_send.at[1, number], kv_recv.at[1, number],
            device_id=(shard(distance), me), device_id_type=MESH,
        )
        copy.start()
        sends.append(copy)

    local[0].wait()
    local[1].wait()
    docs = lens.shape[1]
    square = (docs, docs)
    by_sublane = lax.broadcasted_iota(jnp.int32, square, 0)
    by_lane = lax.broadcasted_iota(jnp.int32, square, 1)
    doc_len = jnp.transpose(jnp.broadcast_to(lens[...], square))
    doc_prefix = jnp.transpose(jnp.broadcast_to(pres[...], square))
    start_row = jnp.sum(jnp.where(by_sublane < by_lane, doc_len, 0), axis=0, keepdims=True)
    doc_start = jnp.transpose(jnp.broadcast_to(start_row, square))
    bounds = []
    for block in range(rows // docs):
        positions = seq * tokens + block * (docs // GROUP) + (by_lane[:1] >> 3)
        bounds.append(key_interval(positions, doc_len, doc_prefix, doc_start))

    local[2].wait()
    local[3].wait()
    for number in range(3):
        sends[number].wait_recv()
    k_all = kbuf[...].reshape(TILES * tokens, -1)
    key_pos = (seq - 2) * tokens + lax.broadcasted_iota(jnp.int32, (TILES * tokens, width), 0)
    per_chunk = width // docs
    for chunk in range(chips):
        at = pl.ds(chunk * width, width)
        block = qbuf[pl.ds(chunk * (width // GROUP), width // GROUP)].astype(jnp.float32)
        q_chunk = block.reshape(width, -1).astype(jnp.bfloat16)
        q2[at, :] = q_chunk
        low, high = (
            jnp.concatenate([b[side] for b in bounds[chunk * per_chunk:(chunk + 1) * per_chunk]], axis=1)
            for side in (0, 1)
        )
        scores = lax.dot_general(k_all, q_chunk, NT, preferred_element_type=jnp.float32)
        scores = jnp.where((key_pos >= low) & (key_pos < high), scores, -1e30)
        top = jnp.max(scores, axis=0, keepdims=True)
        expo = jnp.exp2((scores - top) * (scale * LOG2E))
        chunk_probs = expo * (1.0 / jnp.sum(expo, axis=0, keepdims=True))
        probs[:, at] = chunk_probs
        probs_half[:, at] = chunk_probs.astype(jnp.bfloat16)

    def send_parts(which, total):
        for number, (slot, distance) in enumerate(((0, -2), (1, -1), (3, 1))):
            part_out[which, number] = total[slot * tokens:(slot + 1) * tokens].astype(jnp.bfloat16)
            copy = pltpu.make_async_remote_copy(
                part_out.at[which, number], part_in.at[which, number],
                part_send.at[which, number], part_recv.at[which, number],
                device_id=(shard(distance), me), device_id_type=MESH,
            )
            copy.start()
            parts.append(copy)
        own[which] = total[2 * tokens:3 * tokens]

    parts = []
    for k in range(n_kvh):
        pltpu.make_async_copy(cot.at[k], cot.at[k], cot_recv.at[k]).wait()
        block = cot[k].astype(jnp.float32).reshape(piece, -1)
        c2[pl.ds(k * piece, piece), :] = block.astype(jnp.bfloat16)
    send_parts(0, jnp.dot(probs_half[...], c2[...], preferred_element_type=jnp.float32))

    local[4].wait()
    for number in range(3):
        sends[len(sends) - 3 + number].wait_recv()
    v_all = vbuf[...].reshape(TILES * tokens, -1)
    k_turned = jnp.transpose(k_all.astype(jnp.float32)).astype(jnp.bfloat16)
    queries = []
    for step, d in enumerate((2, 1, 3, 0)):
        target = lax.rem(chip + d, chips)
        at = pl.ds(pl.multiple_of(target * width, width), width)
        dprobs = lax.dot_general(v_all, c2[at, :], NT, preferred_element_type=jnp.float32)
        chunk_probs = probs[:, at]
        delta = jnp.sum(chunk_probs * dprobs, axis=0, keepdims=True)
        ds_chunk = (chunk_probs * (dprobs - delta)).astype(jnp.bfloat16)
        dscores[:, at] = ds_chunk
        turned = jnp.dot(k_turned, ds_chunk, preferred_element_type=jnp.float32)
        block = (jnp.transpose(turned) * scale).reshape(2, piece // GROUP, GROUP, -1)
        gqbuf[pl.ds(2 * target, 2)] = block.astype(jnp.bfloat16)
        if d == 0:
            copy = pltpu.make_async_copy(gqbuf.at[me], gq_out.at[:, me], gq_recv.at[me])
            copy.start()
            holders = [partner]
        else:
            holders = [2 * target, 2 * target + 1]
        for core, holder in enumerate(holders):
            copy = pltpu.make_async_remote_copy(
                gqbuf.at[holder], gq_out.at[:, me], gq_send.at[2 * step + core], gq_recv.at[me],
                device_id=(seq, holder), device_id_type=MESH,
            )
            copy.start()
            queries.append(copy)

    send_parts(1, jnp.dot(dscores[...], q2[...], preferred_element_type=jnp.float32) * scale)

    outs = []
    for which, out in ((0, gv_out), (1, gk_out)):
        total = own[which]
        for number in range(3):
            parts[3 * which + number].wait_recv()
            total = total + part_in[which, number].astype(jnp.float32)
        final[which] = total.astype(jnp.bfloat16)
        copy = pltpu.make_async_copy(final.at[which], out, out_sem.at[which])
        copy.start()
        outs.append(copy)
    for k in range(n_kvh):
        pltpu.make_async_copy(gqbuf.at[k], gq_out.at[:, k], gq_recv.at[k]).wait()
    for copy in sends + parts + queries:
        copy.wait_send()
    for copy in outs:
        copy.wait()


def solution(mesh):
    n_seq, n_kvh = mesh.shape["seq"], mesh.shape["kvh"]

    def step(queries, keys, values, output_gradient, doc_lengths, prefix_lengths):
        tokens, heads, size = queries.shape
        mine = output_gradient.shape[0]
        rows = tokens * heads
        bf16, f32, docs = jnp.bfloat16, jnp.float32, doc_lengths.shape[0]
        anywhere = pl.BlockSpec(memory_space=pl.ANY)
        dma = pltpu.SemaphoreType.DMA
        gq, gk, gv = pl.pallas_call(
            functools.partial(kernel, n_seq, n_kvh, size ** -0.5),
            out_shape=(
                jax.ShapeDtypeStruct((mine, n_kvh, heads, size), bf16),
                jax.ShapeDtypeStruct((tokens, size), bf16),
                jax.ShapeDtypeStruct((tokens, size), bf16),
            ),
            in_specs=[anywhere] * 6,
            out_specs=(anywhere,) * 3,
            scratch_shapes=[
                pltpu.VMEM((tokens, heads, size), bf16),
                pltpu.VMEM((TILES, tokens, size), bf16),
                pltpu.VMEM((TILES, tokens, size), bf16),
                pltpu.VMEM((n_kvh, mine, heads, size), bf16),
                pltpu.VMEM((1, docs), jnp.int32),
                pltpu.VMEM((1, docs), jnp.int32),
                pltpu.VMEM((rows, size), bf16),
                pltpu.VMEM((rows, size), bf16),
                pltpu.VMEM((TILES * tokens, rows), f32),
                pltpu.VMEM((TILES * tokens, rows), bf16),
                pltpu.VMEM((TILES * tokens, rows), bf16),
                pltpu.VMEM((n_kvh, mine, heads, size), bf16),
                pltpu.VMEM((2, 3, tokens, size), bf16),
                pltpu.VMEM((2, 3, tokens, size), bf16),
                pltpu.VMEM((2, tokens, size), f32),
                pltpu.VMEM((2, tokens, size), bf16),
                dma((5,)),
                dma((2, 3)),
                dma((2, 3)),
                dma((n_kvh,)),
                dma((n_kvh,)),
                dma((n_kvh,)),
                dma((n_kvh,)),
                dma((2, 3)),
                dma((2, 3)),
                dma((2,)),
            ],
            compiler_params=pltpu.CompilerParams(collective_id=0, has_side_effects=True),
        )(
            queries,
            keys.reshape(tokens, size),
            values.reshape(tokens, size),
            output_gradient.reshape(mine, n_kvh, heads, size),
            doc_lengths.reshape(1, docs),
            prefix_lengths.reshape(1, docs),
        )
        return gq.reshape(mine, n_kvh * heads, size), gk.reshape(tokens, 1, size), gv.reshape(tokens, 1, size)

    return jax.shard_map(
        step,
        mesh=mesh,
        in_specs=(P("seq", "kvh", None),) * 3 + (P(("seq", "kvh"), None, None), P(), P()),
        out_specs=(P(("seq", "kvh"), None, None), P("seq", "kvh", None), P("seq", "kvh", None)),
        check_vma=False,
    )
```

```python
import functools

import jax
import jax.numpy as jnp
from jax import lax
from jax.experimental import pallas as pl
from jax.experimental.pallas import tpu as pltpu
from jax.sharding import PartitionSpec as P

MESH = pl.DeviceIdType.MESH
GROUP = 8
TILES = 4
LOG2E = 1.4426950408889634
NT = (((1,), (1,)), ((), ()))


def key_interval(positions, doc_len, doc_prefix, doc_start):
    start = jnp.max(jnp.where(doc_start <= positions, doc_start, 0), axis=0, keepdims=True)
    mine = doc_start == start
    length = jnp.sum(jnp.where(mine, doc_len, 0), axis=0, keepdims=True)
    prefix = jnp.sum(jnp.where(mine, doc_prefix, 0), axis=0, keepdims=True)
    stop = jnp.minimum(start + length, jnp.maximum(positions + 1, start + prefix))
    return start, stop


def kernel(
    n_seq, n_kvh, scale,
    q_hbm, k_hbm, v_hbm, og_hbm, len_hbm, pre_hbm,
    gq_out, gk_out, gv_out,
    qbuf, kbuf, vbuf, cot, lens, pres, q2, c2, probs, probs_half, dscores, gqbuf,
    part_out, part_in, own, final,
    local_sem, kv_send, kv_recv, cot_send, cot_recv, gq_send, gq_recv, part_send, part_recv, out_sem,
):
    seq = lax.axis_index("seq")
    me = lax.axis_index("kvh")
    chip = me // 2
    chips = n_kvh // 2
    partner = me + 1 - 2 * lax.rem(me, 2)
    rows = q2.shape[0]
    tokens = kbuf.shape[1]
    piece = rows // n_kvh
    width = 2 * piece

    def inside(distance):
        return (seq + distance >= 0) & (seq + distance < n_seq)

    barrier = pltpu.get_barrier_semaphore()
    for d in range(1, n_kvh):
        other = (seq, lax.rem(me + d, n_kvh))
        pl.semaphore_signal(barrier, inc=1, device_id=other, device_id_type=MESH)
    for d in (-2, -1, 1, 2):
        @pl.when(inside(d))
        def _(d=d):
            pl.semaphore_signal(barrier, inc=1, device_id=(seq + d, me), device_id_type=MESH)

    local = [
        pltpu.make_async_copy(len_hbm, lens, local_sem.at[0]),
        pltpu.make_async_copy(pre_hbm, pres, local_sem.at[1]),
        pltpu.make_async_copy(q_hbm, qbuf, local_sem.at[2]),
        pltpu.make_async_copy(k_hbm, kbuf.at[2], local_sem.at[3]),
        pltpu.make_async_copy(v_hbm, vbuf.at[2], local_sem.at[4]),
        pltpu.make_async_copy(og_hbm.at[:, me], cot.at[me], cot_recv.at[me]),
    ]
    for copy in local:
        copy.start()
    halo = ((2, 0), (1, 1), (-1, 3))
    for number, (distance, slot) in enumerate(halo):
        @pl.when(jnp.logical_not(inside(-distance)))
        def _(slot=slot):
            kbuf[slot] = jnp.zeros_like(kbuf[slot])
            vbuf[slot] = jnp.zeros_like(vbuf[slot])

        @pl.when(jnp.logical_not(inside(distance)))
        def _(number=number):
            part_in[:, number] = jnp.zeros_like(part_in[:, number])
    pl.semaphore_wait(barrier, n_kvh - 1 + sum(inside(d).astype(jnp.int32) for d in (-2, -1, 1, 2)))

    def halo_copy(which, number):
        distance, slot = halo[number]
        source, target = ((k_hbm, kbuf), (v_hbm, vbuf))[which]
        return pltpu.make_async_remote_copy(
            source, target.at[slot], kv_send.at[which, number], kv_recv.at[which, number],
            device_id=(seq + distance, me), device_id_type=MESH,
        )

    def part_copy(which, number):
        distance, _ = halo[number]
        return pltpu.make_async_remote_copy(
            part_out.at[which, number], part_in.at[which, number],
            part_send.at[which, number], part_recv.at[which, number],
            device_id=(seq - distance, me), device_id_type=MESH,
        )

    def each_halo(sign, act):
        for number, (distance, _) in enumerate(halo):
            pl.when(inside(sign * distance))(functools.partial(act, number))

    each_halo(1, lambda number: halo_copy(0, number).start())
    sends = []
    targets = [2 * lax.rem(chip + d, chips) + core for d in (2, 1, 3) for core in (0, 1)]
    targets.append(partner)
    for number, target in enumerate(targets):
        copy = pltpu.make_async_remote_copy(
            og_hbm.at[:, target], cot.at[me], cot_send.at[number], cot_recv.at[me],
            device_id=(seq, target), device_id_type=MESH,
        )
        copy.start()
        sends.append(copy)
    each_halo(1, lambda number: halo_copy(1, number).start())

    local[0].wait()
    local[1].wait()
    docs = lens.shape[1]
    square = (docs, docs)
    by_sublane = lax.broadcasted_iota(jnp.int32, square, 0)
    by_lane = lax.broadcasted_iota(jnp.int32, square, 1)
    doc_len = jnp.transpose(jnp.broadcast_to(lens[...], square))
    doc_prefix = jnp.transpose(jnp.broadcast_to(pres[...], square))
    start_row = jnp.sum(jnp.where(by_sublane < by_lane, doc_len, 0), axis=0, keepdims=True)
    doc_start = jnp.transpose(jnp.broadcast_to(start_row, square))
    bounds = []
    for block in range(rows // docs):
        positions = seq * tokens + block * (docs // GROUP) + (by_lane[:1] >> 3)
        bounds.append(key_interval(positions, doc_len, doc_prefix, doc_start))

    local[2].wait()
    local[3].wait()
    each_halo(-1, lambda number: halo_copy(0, number).wait_recv())
    k_all = kbuf[...].reshape(TILES * tokens, -1)
    key_pos = (seq - 2) * tokens + lax.broadcasted_iota(jnp.int32, (TILES * tokens, width), 0)
    per_chunk = width // docs
    for chunk in range(chips):
        at = pl.ds(chunk * width, width)
        block = qbuf[pl.ds(chunk * (width // GROUP), width // GROUP)].astype(jnp.float32)
        q_chunk = block.reshape(width, -1).astype(jnp.bfloat16)
        q2[at, :] = q_chunk
        low, high = (
            jnp.concatenate([b[side] for b in bounds[chunk * per_chunk:(chunk + 1) * per_chunk]], axis=1)
            for side in (0, 1)
        )
        scores = lax.dot_general(k_all, q_chunk, NT, preferred_element_type=jnp.float32)
        scores = jnp.where((key_pos >= low) & (key_pos < high), scores, -1e30)
        top = jnp.max(scores, axis=0, keepdims=True)
        expo = jnp.exp2((scores - top) * (scale * LOG2E))
        chunk_probs = expo * (1.0 / jnp.sum(expo, axis=0, keepdims=True))
        probs[:, at] = chunk_probs
        probs_half[:, at] = chunk_probs.astype(jnp.bfloat16)

    def send_parts(which, total):
        for number, (_, slot) in enumerate(halo):
            part_out[which, number] = total[slot * tokens:(slot + 1) * tokens].astype(jnp.bfloat16)
        each_halo(-1, lambda number: part_copy(which, number).start())
        own[which] = total[2 * tokens:3 * tokens]

    for k in range(n_kvh):
        pltpu.make_async_copy(cot.at[k], cot.at[k], cot_recv.at[k]).wait()
        block = cot[k].astype(jnp.float32).reshape(piece, -1)
        c2[pl.ds(k * piece, piece), :] = block.astype(jnp.bfloat16)
    send_parts(0, jnp.dot(probs_half[...], c2[...], preferred_element_type=jnp.float32))

    local[4].wait()
    each_halo(-1, lambda number: halo_copy(1, number).wait_recv())
    v_all = vbuf[...].reshape(TILES * tokens, -1)
    k_turned = jnp.transpose(k_all.astype(jnp.float32)).astype(jnp.bfloat16)
    queries = []
    for step, d in enumerate((2, 1, 3, 0)):
        target = lax.rem(chip + d, chips)
        at = pl.ds(pl.multiple_of(target * width, width), width)
        dprobs = lax.dot_general(v_all, c2[at, :], NT, preferred_element_type=jnp.float32)
        chunk_probs = probs[:, at]
        delta = jnp.sum(chunk_probs * dprobs, axis=0, keepdims=True)
        ds_chunk = (chunk_probs * (dprobs - delta)).astype(jnp.bfloat16)
        dscores[:, at] = ds_chunk
        turned = jnp.dot(k_turned, ds_chunk, preferred_element_type=jnp.float32)
        block = (jnp.transpose(turned) * scale).reshape(2, piece // GROUP, GROUP, -1)
        gqbuf[pl.ds(2 * target, 2)] = block.astype(jnp.bfloat16)
        if d == 0:
            copy = pltpu.make_async_copy(gqbuf.at[me], gq_out.at[:, me], gq_recv.at[me])
            copy.start()
            holders = [partner]
        else:
            holders = [2 * target, 2 * target + 1]
        for core, holder in enumerate(holders):
            copy = pltpu.make_async_remote_copy(
                gqbuf.at[holder], gq_out.at[:, me], gq_send.at[2 * step + core], gq_recv.at[me],
                device_id=(seq, holder), device_id_type=MESH,
            )
            copy.start()
            queries.append(copy)

    send_parts(1, jnp.dot(dscores[...], q2[...], preferred_element_type=jnp.float32) * scale)

    outs = []
    for which, out in ((0, gv_out), (1, gk_out)):
        total = own[which]
        each_halo(1, lambda number: part_copy(which, number).wait_recv())
        for number in range(3):
            total = total + part_in[which, number].astype(jnp.float32)
        final[which] = total.astype(jnp.bfloat16)
        copy = pltpu.make_async_copy(final.at[which], out, out_sem.at[which])
        copy.start()
        outs.append(copy)
    for k in range(n_kvh):
        pltpu.make_async_copy(gqbuf.at[k], gq_out.at[:, k], gq_recv.at[k]).wait()
    for which in (0, 1):
        each_halo(1, lambda number: halo_copy(which, number).wait_send())
        each_halo(-1, lambda number: part_copy(which, number).wait_send())
    for copy in sends + queries:
        copy.wait_send()
    for copy in outs:
        copy.wait()


def solution(mesh):
    n_seq, n_kvh = mesh.shape["seq"], mesh.shape["kvh"]

    def step(queries, keys, values, output_gradient, doc_lengths, prefix_lengths):
        tokens, heads, size = queries.shape
        mine = output_gradient.shape[0]
        rows = tokens * heads
        bf16, f32, docs = jnp.bfloat16, jnp.float32, doc_lengths.shape[0]
        anywhere = pl.BlockSpec(memory_space=pl.ANY)
        dma = pltpu.SemaphoreType.DMA
        gq, gk, gv = pl.pallas_call(
            functools.partial(kernel, n_seq, n_kvh, size ** -0.5),
            out_shape=(
                jax.ShapeDtypeStruct((mine, n_kvh, heads, size), bf16),
                jax.ShapeDtypeStruct((tokens, size), bf16),
                jax.ShapeDtypeStruct((tokens, size), bf16),
            ),
            in_specs=[anywhere] * 6,
            out_specs=(anywhere,) * 3,
            scratch_shapes=[
                pltpu.VMEM((tokens, heads, size), bf16),
                pltpu.VMEM((TILES, tokens, size), bf16),
                pltpu.VMEM((TILES, tokens, size), bf16),
                pltpu.VMEM((n_kvh, mine, heads, size), bf16),
                pltpu.VMEM((1, docs), jnp.int32),
                pltpu.VMEM((1, docs), jnp.int32),
                pltpu.VMEM((rows, size), bf16),
                pltpu.VMEM((rows, size), bf16),
                pltpu.VMEM((TILES * tokens, rows), f32),
                pltpu.VMEM((TILES * tokens, rows), bf16),
                pltpu.VMEM((TILES * tokens, rows), bf16),
                pltpu.VMEM((n_kvh, mine, heads, size), bf16),
                pltpu.VMEM((2, 3, tokens, size), bf16),
                pltpu.VMEM((2, 3, tokens, size), bf16),
                pltpu.VMEM((2, tokens, size), f32),
                pltpu.VMEM((2, tokens, size), bf16),
                dma((5,)),
                dma((2, 3)),
                dma((2, 3)),
                dma((n_kvh,)),
                dma((n_kvh,)),
                dma((n_kvh,)),
                dma((n_kvh,)),
                dma((2, 3)),
                dma((2, 3)),
                dma((2,)),
            ],
            compiler_params=pltpu.CompilerParams(collective_id=0, has_side_effects=True),
        )(
            queries,
            keys.reshape(tokens, size),
            values.reshape(tokens, size),
            output_gradient.reshape(mine, n_kvh, heads, size),
            doc_lengths.reshape(1, docs),
            prefix_lengths.reshape(1, docs),
        )
        return gq.reshape(mine, n_kvh * heads, size), gk.reshape(tokens, 1, size), gv.reshape(tokens, 1, size)

    return jax.shard_map(
        step,
        mesh=mesh,
        in_specs=(P("seq", "kvh", None),) * 3 + (P(("seq", "kvh"), None, None), P(), P()),
        out_specs=(P(("seq", "kvh"), None, None), P("seq", "kvh", None), P("seq", "kvh", None)),
        check_vma=False,
    )
```

```python
import functools

import jax
import jax.numpy as jnp
from jax import lax
from jax.experimental import pallas as pl
from jax.experimental.pallas import tpu as pltpu
from jax.sharding import PartitionSpec as P

MESH = pl.DeviceIdType.MESH
GROUP = 8
TILES = 4
VMEM_LIMIT = 32 << 20
LOG2E = 1.4426950408889634
NT = (((1,), (1,)), ((), ()))


def key_interval(positions, doc_len, doc_prefix, doc_start):
    start = jnp.max(jnp.where(doc_start <= positions, doc_start, 0), axis=0, keepdims=True)
    mine = doc_start == start
    length = jnp.sum(jnp.where(mine, doc_len, 0), axis=0, keepdims=True)
    prefix = jnp.sum(jnp.where(mine, doc_prefix, 0), axis=0, keepdims=True)
    stop = jnp.minimum(start + length, jnp.maximum(positions + 1, start + prefix))
    return start, stop


def kernel(
    n_seq, n_kvh, scale,
    q_hbm, k_hbm, v_hbm, og_hbm, len_hbm, pre_hbm,
    gq_out, gk_out, gv_out,
    qbuf, kbuf, vbuf, cot, lens, pres, q2, c2, probs, probs_half, dscores, gqbuf,
    part_out, part_in, own, final,
    local_sem, kv_send, kv_recv, cot_send, cot_recv, gq_send, gq_recv, part_send, part_recv, out_sem,
):
    seq = lax.axis_index("seq")
    me = lax.axis_index("kvh")
    chip = me // 2
    chips = n_kvh // 2
    partner = me + 1 - 2 * lax.rem(me, 2)
    rows = q2.shape[0]
    tokens = kbuf.shape[1]
    piece = rows // n_kvh
    width = 2 * piece

    def inside(distance):
        return (seq + distance >= 0) & (seq + distance < n_seq)

    barrier = pltpu.get_barrier_semaphore()
    for d in range(1, n_kvh):
        other = (seq, lax.rem(me + d, n_kvh))
        pl.semaphore_signal(barrier, inc=1, device_id=other, device_id_type=MESH)
    for d in (-2, -1):
        @pl.when(inside(d))
        def _(d=d):
            pl.semaphore_signal(barrier, inc=1, device_id=(seq + d, me), device_id_type=MESH)

    local = [
        pltpu.make_async_copy(len_hbm, lens, local_sem.at[0]),
        pltpu.make_async_copy(pre_hbm, pres, local_sem.at[1]),
        pltpu.make_async_copy(q_hbm, qbuf, local_sem.at[2]),
        pltpu.make_async_copy(k_hbm, kbuf.at[2], local_sem.at[3]),
        pltpu.make_async_copy(v_hbm, vbuf.at[2], local_sem.at[4]),
        pltpu.make_async_copy(og_hbm.at[:, me], cot.at[me], cot_recv.at[me]),
    ]
    for copy in local:
        copy.start()
    halo = ((2, 0), (1, 1), (-1, 3))
    for number, (distance, slot) in enumerate(halo):
        @pl.when(jnp.logical_not(inside(-distance)))
        def _(slot=slot):
            kbuf[slot] = jnp.zeros_like(kbuf[slot])
            vbuf[slot] = jnp.zeros_like(vbuf[slot])

        @pl.when(jnp.logical_not(inside(distance)))
        def _(number=number):
            part_in[:, number] = jnp.zeros_like(part_in[:, number])
    pl.semaphore_wait(barrier, n_kvh - 1 + sum(inside(d).astype(jnp.int32) for d in (1, 2)))

    def halo_copy(which, number):
        distance, slot = halo[number]
        source, target = ((k_hbm, kbuf), (v_hbm, vbuf))[which]
        return pltpu.make_async_remote_copy(
            source, target.at[slot], kv_send.at[which, number], kv_recv.at[which, number],
            device_id=(seq + distance, me), device_id_type=MESH,
        )

    def part_copy(which, number):
        distance, _ = halo[number]
        return pltpu.make_async_remote_copy(
            part_out.at[which, number], part_in.at[which, number],
            part_send.at[which, number], part_recv.at[which, number],
            device_id=(seq - distance, me), device_id_type=MESH,
        )

    def each_halo(sign, act):
        for number, (distance, _) in enumerate(halo):
            pl.when(inside(sign * distance))(functools.partial(act, number))

    for number in (0, 1):
        pl.when(inside(halo[number][0]))(lambda number=number: halo_copy(0, number).start())
    sends = []
    targets = [2 * lax.rem(chip + d, chips) + core for d in (2, 1, 3) for core in (0, 1)]
    targets.append(partner)
    for number, target in enumerate(targets):
        copy = pltpu.make_async_remote_copy(
            og_hbm.at[:, target], cot.at[me], cot_send.at[number], cot_recv.at[me],
            device_id=(seq, target), device_id_type=MESH,
        )
        copy.start()
        sends.append(copy)
    for number in (0, 1):
        pl.when(inside(halo[number][0]))(lambda number=number: halo_copy(1, number).start())

    local[0].wait()
    local[1].wait()
    docs = lens.shape[1]
    square = (docs, docs)
    by_sublane = lax.broadcasted_iota(jnp.int32, square, 0)
    by_lane = lax.broadcasted_iota(jnp.int32, square, 1)
    doc_len = jnp.transpose(jnp.broadcast_to(lens[...], square))
    doc_prefix = jnp.transpose(jnp.broadcast_to(pres[...], square))
    start_row = jnp.sum(jnp.where(by_sublane < by_lane, doc_len, 0), axis=0, keepdims=True)
    doc_start = jnp.transpose(jnp.broadcast_to(start_row, square))
    bounds = []
    for block in range(rows // docs):
        positions = seq * tokens + block * (docs // GROUP) + (by_lane[:1] >> 3)
        bounds.append(key_interval(positions, doc_len, doc_prefix, doc_start))

    local[2].wait()
    local[3].wait()

    @pl.when(inside(-1))
    def _():
        halo_copy(0, 1).wait_recv()
        halo_copy(0, 2).start()
        halo_copy(1, 2).start()
    for number in (0, 2):
        pl.when(inside(-halo[number][0]))(lambda number=number: halo_copy(0, number).wait_recv())
    k_all = kbuf[...].reshape(TILES * tokens, -1)
    key_pos = (seq - 2) * tokens + lax.broadcasted_iota(jnp.int32, (TILES * tokens, width), 0)
    per_chunk = width // docs
    for chunk in range(chips):
        at = pl.ds(chunk * width, width)
        block = qbuf[pl.ds(chunk * (width // GROUP), width // GROUP)].astype(jnp.float32)
        q_chunk = block.reshape(width, -1).astype(jnp.bfloat16)
        q2[at, :] = q_chunk
        low, high = (
            jnp.concatenate([b[side] for b in bounds[chunk * per_chunk:(chunk + 1) * per_chunk]], axis=1)
            for side in (0, 1)
        )
        scores = lax.dot_general(k_all, q_chunk, NT, preferred_element_type=jnp.float32)
        scores = jnp.where((key_pos >= low) & (key_pos < high), scores, -1e30)
        top = jnp.max(scores, axis=0, keepdims=True)
        expo = jnp.exp2((scores - top) * (scale * LOG2E))
        chunk_probs = expo * (1.0 / jnp.sum(expo, axis=0, keepdims=True))
        probs[:, at] = chunk_probs
        probs_half[:, at] = chunk_probs.astype(jnp.bfloat16)

    def send_parts(which, total):
        for number, (_, slot) in enumerate(halo):
            part_out[which, number] = total[slot * tokens:(slot + 1) * tokens].astype(jnp.bfloat16)
        each_halo(-1, lambda number: part_copy(which, number).start())
        own[which] = total[2 * tokens:3 * tokens]

    for k in range(n_kvh):
        pltpu.make_async_copy(cot.at[k], cot.at[k], cot_recv.at[k]).wait()
        block = cot[k].astype(jnp.float32).reshape(piece, -1)
        c2[pl.ds(k * piece, piece), :] = block.astype(jnp.bfloat16)
    send_parts(0, jnp.dot(probs_half[...], c2[...], preferred_element_type=jnp.float32))

    local[4].wait()
    each_halo(-1, lambda number: halo_copy(1, number).wait_recv())
    v_all = vbuf[...].reshape(TILES * tokens, -1)
    k_turned = jnp.transpose(k_all.astype(jnp.float32)).astype(jnp.bfloat16)
    queries = []
    for step, d in enumerate((2, 1, 3, 0)):
        target = lax.rem(chip + d, chips)
        at = pl.ds(pl.multiple_of(target * width, width), width)
        dprobs = lax.dot_general(v_all, c2[at, :], NT, preferred_element_type=jnp.float32)
        chunk_probs = probs[:, at]
        delta = jnp.sum(chunk_probs * dprobs, axis=0, keepdims=True)
        ds_chunk = (chunk_probs * (dprobs - delta)).astype(jnp.bfloat16)
        dscores[:, at] = ds_chunk
        turned = jnp.dot(k_turned, ds_chunk, preferred_element_type=jnp.float32)
        block = (jnp.transpose(turned) * scale).reshape(2, piece // GROUP, GROUP, -1)
        gqbuf[pl.ds(2 * target, 2)] = block.astype(jnp.bfloat16)
        if d == 0:
            copy = pltpu.make_async_copy(gqbuf.at[me], gq_out.at[:, me], gq_recv.at[me])
            copy.start()
            holders = [partner]
        else:
            holders = [2 * target, 2 * target + 1]
        for core, holder in enumerate(holders):
            copy = pltpu.make_async_remote_copy(
                gqbuf.at[holder], gq_out.at[:, me], gq_send.at[2 * step + core], gq_recv.at[me],
                device_id=(seq, holder), device_id_type=MESH,
            )
            copy.start()
            queries.append(copy)

    send_parts(1, jnp.dot(dscores[...], q2[...], preferred_element_type=jnp.float32) * scale)

    outs = []
    for which, out in ((0, gv_out), (1, gk_out)):
        total = own[which]
        each_halo(1, lambda number: part_copy(which, number).wait_recv())
        for number in range(3):
            total = total + part_in[which, number].astype(jnp.float32)
        final[which] = total.astype(jnp.bfloat16)
        copy = pltpu.make_async_copy(final.at[which], out, out_sem.at[which])
        copy.start()
        outs.append(copy)
    for k in range(n_kvh):
        pltpu.make_async_copy(gqbuf.at[k], gq_out.at[:, k], gq_recv.at[k]).wait()
    for which in (0, 1):
        each_halo(1, lambda number: halo_copy(which, number).wait_send())
        each_halo(-1, lambda number: part_copy(which, number).wait_send())
    for copy in sends + queries:
        copy.wait_send()
    for copy in outs:
        copy.wait()


def finish(gq_in, gk_in, gv_in, gq_out, gk_out, gv_out, sem):
    copies = [
        pltpu.make_async_copy(source, target, sem.at[number])
        for number, (source, target) in enumerate(((gq_in, gq_out), (gk_in, gk_out), (gv_in, gv_out)))
    ]
    for copy in copies:
        copy.start()
    for copy in copies:
        copy.wait()


def solution(mesh):
    n_seq, n_kvh = mesh.shape["seq"], mesh.shape["kvh"]

    def step(queries, keys, values, output_gradient, doc_lengths, prefix_lengths):
        tokens, heads, size = queries.shape
        mine = output_gradient.shape[0]
        rows = tokens * heads
        bf16, f32, docs = jnp.bfloat16, jnp.float32, doc_lengths.shape[0]
        anywhere = pl.BlockSpec(memory_space=pl.ANY)
        dma = pltpu.SemaphoreType.DMA
        shapes = (
            jax.ShapeDtypeStruct((mine, n_kvh, heads, size), bf16),
            jax.ShapeDtypeStruct((tokens, size), bf16),
            jax.ShapeDtypeStruct((tokens, size), bf16),
        )
        results = pl.pallas_call(
            functools.partial(kernel, n_seq, n_kvh, size ** -0.5),
            out_shape=shapes,
            in_specs=[pl.BlockSpec(memory_space=pltpu.HBM)] * 6,
            out_specs=(anywhere,) * 3,
            scratch_shapes=[
                pltpu.VMEM((tokens, heads, size), bf16),
                pltpu.VMEM((TILES, tokens, size), bf16),
                pltpu.VMEM((TILES, tokens, size), bf16),
                pltpu.VMEM((n_kvh, mine, heads, size), bf16),
                pltpu.VMEM((1, docs), jnp.int32),
                pltpu.VMEM((1, docs), jnp.int32),
                pltpu.VMEM((rows, size), bf16),
                pltpu.VMEM((rows, size), bf16),
                pltpu.VMEM((TILES * tokens, rows), f32),
                pltpu.VMEM((TILES * tokens, rows), bf16),
                pltpu.VMEM((TILES * tokens, rows), bf16),
                pltpu.VMEM((n_kvh, mine, heads, size), bf16),
                pltpu.VMEM((2, 3, tokens, size), bf16),
                pltpu.VMEM((2, 3, tokens, size), bf16),
                pltpu.VMEM((2, tokens, size), f32),
                pltpu.VMEM((2, tokens, size), bf16),
                dma((5,)),
                dma((2, 3)),
                dma((2, 3)),
                dma((n_kvh,)),
                dma((n_kvh,)),
                dma((n_kvh,)),
                dma((n_kvh,)),
                dma((2, 3)),
                dma((2, 3)),
                dma((2,)),
            ],
            compiler_params=pltpu.CompilerParams(collective_id=0, has_side_effects=True, vmem_limit_bytes=VMEM_LIMIT),
        )(*(pltpu.with_memory_space_constraint(x, pltpu.HBM) for x in (
            queries,
            keys.reshape(tokens, size),
            values.reshape(tokens, size),
            output_gradient.reshape(mine, n_kvh, heads, size),
            doc_lengths.reshape(1, docs),
            prefix_lengths.reshape(1, docs),
        )))
        gq, gk, gv = pl.pallas_call(
            finish,
            out_shape=shapes,
            in_specs=[anywhere] * 3,
            out_specs=(pl.BlockSpec(memory_space=pltpu.HBM),) * 3,
            scratch_shapes=[dma((3,))],
            compiler_params=pltpu.CompilerParams(vmem_limit_bytes=1 << 20),
        )(*results)
        return gq.reshape(mine, n_kvh * heads, size), gk.reshape(tokens, 1, size), gv.reshape(tokens, 1, size)

    return jax.shard_map(
        step,
        mesh=mesh,
        in_specs=(P("seq", "kvh", None),) * 3 + (P(("seq", "kvh"), None, None), P(), P()),
        out_specs=(P(("seq", "kvh"), None, None), P("seq", "kvh", None), P("seq", "kvh", None)),
        check_vma=False,
    )
```

```python
import functools

import jax
import jax.numpy as jnp
from jax import lax
from jax.experimental import pallas as pl
from jax.experimental.pallas import tpu as pltpu
from jax.sharding import PartitionSpec as P

MESH = pl.DeviceIdType.MESH
GROUP = 8
TILES = 4
VMEM_LIMIT = 32 << 20
LOG2E = 1.4426950408889634
NT = (((1,), (1,)), ((), ()))


def key_interval(positions, doc_len, doc_prefix, doc_start):
    start = jnp.max(jnp.where(doc_start <= positions, doc_start, 0), axis=0, keepdims=True)
    mine = doc_start == start
    length = jnp.sum(jnp.where(mine, doc_len, 0), axis=0, keepdims=True)
    prefix = jnp.sum(jnp.where(mine, doc_prefix, 0), axis=0, keepdims=True)
    stop = jnp.minimum(start + length, jnp.maximum(positions + 1, start + prefix))
    return start, stop


def kernel(
    n_seq, n_kvh, scale,
    q_hbm, k_hbm, v_hbm, og_hbm, len_hbm, pre_hbm,
    gq_out, gk_out, gv_out,
    qbuf, kbuf, vbuf, cot, lens, pres, q2, c2, probs, probs_half, gqbuf,
    part_out, part_in, own, final,
    local_sem, kv_send, kv_recv, cot_send, cot_recv, gq_send, gq_recv, part_send, part_recv, out_sem, ready,
):
    seq = lax.axis_index("seq")
    me = lax.axis_index("kvh")
    chip = me // 2
    chips = n_kvh // 2
    partner = me + 1 - 2 * lax.rem(me, 2)
    rows = q2.shape[0]
    tokens = kbuf.shape[1]
    piece = rows // n_kvh
    width = 2 * piece

    def inside(distance):
        return (seq + distance >= 0) & (seq + distance < n_seq)

    barrier = pltpu.get_barrier_semaphore()
    for d in range(1, n_kvh):
        other = (seq, lax.rem(me + d, n_kvh))
        pl.semaphore_signal(barrier, inc=1, device_id=other, device_id_type=MESH)
    for d in (-2, -1):
        @pl.when(inside(d))
        def _(d=d):
            pl.semaphore_signal(barrier, inc=1, device_id=(seq + d, me), device_id_type=MESH)

    local = [
        pltpu.make_async_copy(len_hbm, lens, local_sem.at[0]),
        pltpu.make_async_copy(pre_hbm, pres, local_sem.at[1]),
        pltpu.make_async_copy(q_hbm, qbuf, local_sem.at[2]),
        pltpu.make_async_copy(k_hbm, kbuf.at[2], local_sem.at[3]),
        pltpu.make_async_copy(v_hbm, vbuf.at[2], local_sem.at[4]),
        pltpu.make_async_copy(og_hbm.at[:, me], cot.at[me], cot_recv.at[me]),
    ]
    for copy in local:
        copy.start()
    halo = ((2, 0), (1, 1), (-1, 3))
    for number, (distance, slot) in enumerate(halo):
        @pl.when(jnp.logical_not(inside(-distance)))
        def _(slot=slot):
            kbuf[slot] = jnp.zeros_like(kbuf[slot])
            vbuf[slot] = jnp.zeros_like(vbuf[slot])

        @pl.when(jnp.logical_not(inside(distance)))
        def _(number=number):
            part_in[:, number] = jnp.zeros_like(part_in[:, number])
    pl.semaphore_wait(barrier, n_kvh - 1 + sum(inside(d).astype(jnp.int32) for d in (1, 2)))

    def halo_copy(which, number):
        distance, slot = halo[number]
        source, target = ((k_hbm, kbuf), (v_hbm, vbuf))[which]
        return pltpu.make_async_remote_copy(
            source, target.at[slot], kv_send.at[which, number], kv_recv.at[which, number],
            device_id=(seq + distance, me), device_id_type=MESH,
        )

    def part_copy(which, number):
        distance, _ = halo[number]
        return pltpu.make_async_remote_copy(
            part_out.at[which, number], part_in.at[which, number],
            part_send.at[which, number], part_recv.at[which, number],
            device_id=(seq - distance, me), device_id_type=MESH,
        )

    def each_halo(sign, act):
        for number, (distance, _) in enumerate(halo):
            pl.when(inside(sign * distance))(functools.partial(act, number))

    @pl.when(inside(1))
    def _():
        pl.semaphore_signal(ready, inc=1, device_id=(seq + 1, me), device_id_type=MESH)
    for number in (0, 1):
        pl.when(inside(halo[number][0]))(lambda number=number: halo_copy(0, number).start())
    sends = []
    targets = [2 * lax.rem(chip + d, chips) + core for d in (2, 1, 3) for core in (0, 1)]
    targets.append(partner)
    for number, target in enumerate(targets):
        copy = pltpu.make_async_remote_copy(
            og_hbm.at[:, target], cot.at[me], cot_send.at[number], cot_recv.at[me],
            device_id=(seq, target), device_id_type=MESH,
        )
        copy.start()
        sends.append(copy)
    for number in (0, 1):
        pl.when(inside(halo[number][0]))(lambda number=number: halo_copy(1, number).start())

    local[0].wait()
    local[1].wait()
    docs = lens.shape[1]
    square = (docs, docs)
    by_sublane = lax.broadcasted_iota(jnp.int32, square, 0)
    by_lane = lax.broadcasted_iota(jnp.int32, square, 1)
    doc_len = jnp.transpose(jnp.broadcast_to(lens[...], square))
    doc_prefix = jnp.transpose(jnp.broadcast_to(pres[...], square))
    start_row = jnp.sum(jnp.where(by_sublane < by_lane, doc_len, 0), axis=0, keepdims=True)
    doc_start = jnp.transpose(jnp.broadcast_to(start_row, square))
    bounds = []
    for block in range(rows // docs):
        positions = seq * tokens + block * (docs // GROUP) + (by_lane[:1] >> 3)
        bounds.append(key_interval(positions, doc_len, doc_prefix, doc_start))

    local[2].wait()
    local[3].wait()

    @pl.when(inside(-1))
    def _():
        pl.semaphore_wait(ready, 1)
        halo_copy(0, 2).start()
        halo_copy(1, 2).start()
    for number in (0, 1, 2):
        pl.when(inside(-halo[number][0]))(lambda number=number: halo_copy(0, number).wait_recv())
    k_all = kbuf[...].reshape(TILES * tokens, -1)
    key_pos = (seq - 2) * tokens + lax.broadcasted_iota(jnp.int32, (TILES * tokens, width), 0)
    per_chunk = width // docs
    for chunk in range(chips):
        at = pl.ds(chunk * width, width)
        block = qbuf[pl.ds(chunk * (width // GROUP), width // GROUP)].astype(jnp.float32)
        q_chunk = block.reshape(width, -1).astype(jnp.bfloat16)
        q2[at, :] = q_chunk
        low, high = (
            jnp.concatenate([b[side] for b in bounds[chunk * per_chunk:(chunk + 1) * per_chunk]], axis=1)
            for side in (0, 1)
        )
        scores = lax.dot_general(k_all, q_chunk, NT, preferred_element_type=jnp.float32)
        scores = jnp.where((key_pos >= low) & (key_pos < high), scores, -1e30)
        top = jnp.max(scores, axis=0, keepdims=True)
        expo = jnp.exp2((scores - top) * (scale * LOG2E))
        chunk_probs = expo * (1.0 / jnp.sum(expo, axis=0, keepdims=True))
        probs[:, at] = chunk_probs
        probs_half[:, at] = chunk_probs.astype(jnp.bfloat16)

    def store_parts(which, total):
        for number, (_, slot) in enumerate(halo):
            part_out[which, number] = total[slot * tokens:(slot + 1) * tokens].astype(jnp.bfloat16)
        own[which] = total[2 * tokens:3 * tokens]

    def send_parts(which):
        each_halo(-1, lambda number: part_copy(which, number).start())

    local[4].wait()
    each_halo(-1, lambda number: halo_copy(1, number).wait_recv())
    for k in range(n_kvh):
        pltpu.make_async_copy(cot.at[k], cot.at[k], cot_recv.at[k]).wait()
    for k in range(n_kvh):
        block = cot[k].astype(jnp.float32).reshape(piece, -1)
        c2[pl.ds(k * piece, piece), :] = block.astype(jnp.bfloat16)

    order = (2, 1, 3, 0)
    v_all = vbuf[...].reshape(TILES * tokens, -1)
    k_turned = jnp.transpose(k_all.astype(jnp.float32)).astype(jnp.bfloat16)

    def chunk_of(step):
        target = lax.rem(chip + order[step], chips)
        return target, pl.ds(pl.multiple_of(target * width, width), width)

    def score_gradients(step):
        _, at = chunk_of(step)
        dprobs = lax.dot_general(v_all, c2[at, :], NT, preferred_element_type=jnp.float32)
        chunk_probs = probs[:, at]
        delta = jnp.sum(chunk_probs * dprobs, axis=0, keepdims=True)
        return (chunk_probs * (dprobs - delta)).astype(jnp.bfloat16)

    def query_gradients(step, ds_chunk):
        target, _ = chunk_of(step)
        turned = jnp.dot(k_turned, ds_chunk, preferred_element_type=jnp.float32)
        block = (jnp.transpose(turned) * scale).reshape(2, piece // GROUP, GROUP, -1)
        gqbuf[pl.ds(2 * target, 2)] = block.astype(jnp.bfloat16)

    def key_gradients(step, ds_chunk):
        _, at = chunk_of(step)
        return jnp.dot(ds_chunk, q2[at, :], preferred_element_type=jnp.float32)

    queries = []

    def send_queries(step):
        target, _ = chunk_of(step)
        holders = [2 * target, 2 * target + 1] if order[step] else [partner]
        if not order[step]:
            pltpu.make_async_copy(gqbuf.at[me], gq_out.at[:, me], gq_recv.at[me]).start()
        for core, holder in enumerate(holders):
            copy = pltpu.make_async_remote_copy(
                gqbuf.at[holder], gq_out.at[:, me], gq_send.at[2 * step + core], gq_recv.at[me],
                device_id=(seq, holder), device_id_type=MESH,
            )
            copy.start()
            queries.append(copy)

    ds_chunk = score_gradients(0)
    store_parts(0, jnp.dot(probs_half[...], c2[...], preferred_element_type=jnp.float32))
    send_parts(0)
    key_total = None
    for step in range(chips):
        later = score_gradients(step + 1) if step + 1 < chips else None
        query_gradients(step, ds_chunk)
        term = key_gradients(step, ds_chunk)
        key_total = term if key_total is None else key_total + term
        if later is None:
            store_parts(1, key_total * scale)
            send_parts(1)
        send_queries(step)
        ds_chunk = later

    outs = []
    for which, out in ((0, gv_out), (1, gk_out)):
        total = own[which]
        each_halo(1, lambda number: part_copy(which, number).wait_recv())
        for number in range(3):
            total = total + part_in[which, number].astype(jnp.float32)
        final[which] = total.astype(jnp.bfloat16)
        copy = pltpu.make_async_copy(final.at[which], out, out_sem.at[which])
        copy.start()
        outs.append(copy)
    for k in range(n_kvh):
        pltpu.make_async_copy(gqbuf.at[k], gq_out.at[:, k], gq_recv.at[k]).wait()
    for which in (0, 1):
        each_halo(1, lambda number: halo_copy(which, number).wait_send())
        each_halo(-1, lambda number: part_copy(which, number).wait_send())
    for copy in sends + queries:
        copy.wait_send()
    for copy in outs:
        copy.wait()


def finish(gq_in, gk_in, gv_in, gq_out, gk_out, gv_out, sem):
    copies = [
        pltpu.make_async_copy(source, target, sem.at[number])
        for number, (source, target) in enumerate(((gq_in, gq_out), (gk_in, gk_out), (gv_in, gv_out)))
    ]
    for copy in copies:
        copy.start()
    for copy in copies:
        copy.wait()


def solution(mesh):
    n_seq, n_kvh = mesh.shape["seq"], mesh.shape["kvh"]

    def step(queries, keys, values, output_gradient, doc_lengths, prefix_lengths):
        tokens, heads, size = queries.shape
        mine = output_gradient.shape[0]
        rows = tokens * heads
        bf16, f32, docs = jnp.bfloat16, jnp.float32, doc_lengths.shape[0]
        anywhere = pl.BlockSpec(memory_space=pl.ANY)
        dma = pltpu.SemaphoreType.DMA
        shapes = (
            jax.ShapeDtypeStruct((mine, n_kvh, heads, size), bf16),
            jax.ShapeDtypeStruct((tokens, size), bf16),
            jax.ShapeDtypeStruct((tokens, size), bf16),
        )
        results = pl.pallas_call(
            functools.partial(kernel, n_seq, n_kvh, size ** -0.5),
            out_shape=shapes,
            in_specs=[pl.BlockSpec(memory_space=pltpu.HBM)] * 6,
            out_specs=(anywhere,) * 3,
            scratch_shapes=[
                pltpu.VMEM((tokens, heads, size), bf16),
                pltpu.VMEM((TILES, tokens, size), bf16),
                pltpu.VMEM((TILES, tokens, size), bf16),
                pltpu.VMEM((n_kvh, mine, heads, size), bf16),
                pltpu.VMEM((1, docs), jnp.int32),
                pltpu.VMEM((1, docs), jnp.int32),
                pltpu.VMEM((rows, size), bf16),
                pltpu.VMEM((rows, size), bf16),
                pltpu.VMEM((TILES * tokens, rows), f32),
                pltpu.VMEM((TILES * tokens, rows), bf16),
                pltpu.VMEM((n_kvh, mine, heads, size), bf16),
                pltpu.VMEM((2, 3, tokens, size), bf16),
                pltpu.VMEM((2, 3, tokens, size), bf16),
                pltpu.VMEM((2, tokens, size), f32),
                pltpu.VMEM((2, tokens, size), bf16),
                dma((5,)),
                dma((2, 3)),
                dma((2, 3)),
                dma((n_kvh,)),
                dma((n_kvh,)),
                dma((n_kvh,)),
                dma((n_kvh,)),
                dma((2, 3)),
                dma((2, 3)),
                dma((2,)),
                pltpu.SemaphoreType.REGULAR,
            ],
            compiler_params=pltpu.CompilerParams(collective_id=0, has_side_effects=True, vmem_limit_bytes=VMEM_LIMIT),
        )(*(pltpu.with_memory_space_constraint(x, pltpu.HBM) for x in (
            queries,
            keys.reshape(tokens, size),
            values.reshape(tokens, size),
            output_gradient.reshape(mine, n_kvh, heads, size),
            doc_lengths.reshape(1, docs),
            prefix_lengths.reshape(1, docs),
        )))
        gq, gk, gv = pl.pallas_call(
            finish,
            out_shape=shapes,
            in_specs=[anywhere] * 3,
            out_specs=(pl.BlockSpec(memory_space=pltpu.HBM),) * 3,
            scratch_shapes=[dma((3,))],
            compiler_params=pltpu.CompilerParams(vmem_limit_bytes=1 << 20),
        )(*results)
        return gq.reshape(mine, n_kvh * heads, size), gk.reshape(tokens, 1, size), gv.reshape(tokens, 1, size)

    return jax.shard_map(
        step,
        mesh=mesh,
        in_specs=(P("seq", "kvh", None),) * 3 + (P(("seq", "kvh"), None, None), P(), P()),
        out_specs=(P(("seq", "kvh"), None, None), P("seq", "kvh", None), P("seq", "kvh", None)),
        check_vma=False,
    )
```

```python
import functools

import jax
import jax.numpy as jnp
from jax import lax
from jax.experimental import pallas as pl
from jax.experimental.pallas import tpu as pltpu
from jax.sharding import PartitionSpec as P

MESH = pl.DeviceIdType.MESH
GROUP = 8
TILES = 4
OWN = 1
VMEM_LIMIT = 32 << 20
LOG2E = 1.4426950408889634
NT = (((1,), (1,)), ((), ()))


def key_interval(positions, doc_len, doc_prefix, doc_start):
    start = jnp.max(jnp.where(doc_start <= positions, doc_start, 0), axis=0, keepdims=True)
    mine = doc_start == start
    length = jnp.sum(jnp.where(mine, doc_len, 0), axis=0, keepdims=True)
    prefix = jnp.sum(jnp.where(mine, doc_prefix, 0), axis=0, keepdims=True)
    stop = jnp.minimum(start + length, jnp.maximum(positions + 1, start + prefix))
    return start, stop


def kernel(
    n_seq, n_kvh, scale,
    q_hbm, k_hbm, v_hbm, og_hbm, len_hbm, pre_hbm,
    gq_out, gk_out, gv_out,
    qbuf, kbuf, vbuf, cot, lens, pres, q2, c2, probs, probs_half, gqbuf,
    part_out, part_in, own, final,
    local_sem, kv_send, kv_recv, cot_send, cot_recv, gq_send, gq_recv, part_send, part_recv, out_sem, ready,
):
    seq = lax.axis_index("seq")
    me = lax.axis_index("kvh")
    chip = me // 2
    chips = n_kvh // 2
    partner = me + 1 - 2 * lax.rem(me, 2)
    rows = q2.shape[0]
    tokens = kbuf.shape[1]
    piece = rows // n_kvh
    width = 2 * piece

    def inside(distance):
        return (seq + distance >= 0) & (seq + distance < n_seq)

    barrier = pltpu.get_barrier_semaphore()
    for d in range(1, n_kvh):
        other = (seq, lax.rem(me + d, n_kvh))
        pl.semaphore_signal(barrier, inc=1, device_id=other, device_id_type=MESH)
    for d in (-2, -1):
        @pl.when(inside(d))
        def _(d=d):
            pl.semaphore_signal(barrier, inc=1, device_id=(seq + d, me), device_id_type=MESH)

    local = [
        pltpu.make_async_copy(len_hbm, lens, local_sem.at[0]),
        pltpu.make_async_copy(pre_hbm, pres, local_sem.at[1]),
        pltpu.make_async_copy(q_hbm, qbuf, local_sem.at[2]),
        pltpu.make_async_copy(k_hbm, kbuf.at[OWN], local_sem.at[3]),
        pltpu.make_async_copy(v_hbm, vbuf.at[OWN], local_sem.at[4]),
        pltpu.make_async_copy(og_hbm.at[:, me], cot.at[me], cot_recv.at[me]),
    ]
    for copy in local:
        copy.start()
    halo = ((2, 2), (1, 0), (-1, 3))
    for number, (distance, slot) in enumerate(halo):
        @pl.when(jnp.logical_not(inside(-distance)))
        def _(slot=slot):
            kbuf[slot] = jnp.zeros_like(kbuf[slot])
            vbuf[slot] = jnp.zeros_like(vbuf[slot])

        @pl.when(jnp.logical_not(inside(distance)))
        def _(number=number):
            part_in[:, number] = jnp.zeros_like(part_in[:, number])
    pl.semaphore_wait(barrier, n_kvh - 1 + sum(inside(d).astype(jnp.int32) for d in (1, 2)))

    def halo_copy(which, number):
        distance, slot = halo[number]
        source, target = ((k_hbm, kbuf), (v_hbm, vbuf))[which]
        return pltpu.make_async_remote_copy(
            source, target.at[slot], kv_send.at[which, number], kv_recv.at[which, number],
            device_id=(seq + distance, me), device_id_type=MESH,
        )

    def part_copy(which, number):
        distance, _ = halo[number]
        return pltpu.make_async_remote_copy(
            part_out.at[which, number], part_in.at[which, number],
            part_send.at[which, number], part_recv.at[which, number],
            device_id=(seq - distance, me), device_id_type=MESH,
        )

    def each_halo(sign, act):
        for number, (distance, _) in enumerate(halo):
            pl.when(inside(sign * distance))(functools.partial(act, number))

    @pl.when(inside(1))
    def _():
        pl.semaphore_signal(ready, inc=1, device_id=(seq + 1, me), device_id_type=MESH)
    for number in (0, 1):
        pl.when(inside(halo[number][0]))(lambda number=number: halo_copy(0, number).start())
    sends = []
    targets = [2 * lax.rem(chip + d, chips) + core for d in (2, 1, 3) for core in (0, 1)]
    targets.append(partner)
    for number, target in enumerate(targets):
        copy = pltpu.make_async_remote_copy(
            og_hbm.at[:, target], cot.at[me], cot_send.at[number], cot_recv.at[me],
            device_id=(seq, target), device_id_type=MESH,
        )
        copy.start()
        sends.append(copy)
    for number in (0, 1):
        pl.when(inside(halo[number][0]))(lambda number=number: halo_copy(1, number).start())

    @pl.when(inside(-1))
    def _():
        pl.semaphore_wait(ready, 1)
        halo_copy(0, 2).start()
        halo_copy(1, 2).start()

    local[0].wait()
    local[1].wait()
    docs = lens.shape[1]
    square = (docs, docs)
    by_sublane = lax.broadcasted_iota(jnp.int32, square, 0)
    by_lane = lax.broadcasted_iota(jnp.int32, square, 1)
    doc_len = jnp.transpose(jnp.broadcast_to(lens[...], square))
    doc_prefix = jnp.transpose(jnp.broadcast_to(pres[...], square))
    start_row = jnp.sum(jnp.where(by_sublane < by_lane, doc_len, 0), axis=0, keepdims=True)
    doc_start = jnp.transpose(jnp.broadcast_to(start_row, square))
    bounds = []
    for block in range(rows // docs):
        positions = seq * tokens + block * (docs // GROUP) + (by_lane[:1] >> 3)
        bounds.append(key_interval(positions, doc_len, doc_prefix, doc_start))

    tile = (tokens, width)
    key_at = lax.broadcasted_iota(jnp.int32, tile, 0)
    token_at = lax.broadcasted_iota(jnp.int32, tile, 1) >> 3
    factor = scale * LOG2E

    def is_back(chunk):
        return key_at > token_at + chunk * (width // GROUP)

    def hidden(scores, positions, bound):
        return jnp.where((positions >= bound[0]) & (positions < bound[1]), scores, -1e30)

    local[2].wait()
    local[3].wait()
    per_chunk = width // docs
    limits, tops, sums = [], [], []
    for chunk in range(chips):
        at = pl.ds(chunk * width, width)
        block = qbuf[pl.ds(chunk * (width // GROUP), width // GROUP)].astype(jnp.float32)
        q_chunk = block.reshape(width, -1).astype(jnp.bfloat16)
        q2[at, :] = q_chunk
        limits.append([
            jnp.concatenate([b[side] for b in bounds[chunk * per_chunk:(chunk + 1) * per_chunk]], axis=1)
            for side in (0, 1)
        ])
        scores = lax.dot_general(kbuf[OWN], q_chunk, NT, preferred_element_type=jnp.float32)
        scores = hidden(scores, key_at + seq * tokens, limits[chunk])
        tops.append(jnp.max(scores, axis=0, keepdims=True))
        expo = jnp.exp2((scores - tops[chunk]) * factor)
        sums.append(jnp.sum(expo, axis=0, keepdims=True))
        probs[OWN * tokens:(OWN + 1) * tokens, at] = expo

    for number in (0, 1, 2):
        pl.when(inside(-halo[number][0]))(lambda number=number: halo_copy(0, number).wait_recv())
    k_all = kbuf[...].reshape(TILES * tokens, -1)
    for chunk in range(chips):
        at = pl.ds(chunk * width, width)
        back = is_back(chunk)
        before, _, far, ahead = (
            lax.dot_general(kbuf[slot], q2[at, :], NT, preferred_element_type=jnp.float32) if slot != OWN else None
            for slot in range(TILES)
        )
        before = hidden(before, key_at + (seq - 1) * tokens, limits[chunk])
        outer = hidden(
            jnp.where(back, far, ahead),
            key_at + jnp.where(back, (seq - 2) * tokens, (seq + 1) * tokens),
            limits[chunk],
        )
        top = jnp.maximum(tops[chunk], jnp.max(jnp.maximum(before, outer), axis=0, keepdims=True))
        before = jnp.exp2((before - top) * factor)
        outer = jnp.exp2((outer - top) * factor)
        shrink = jnp.exp2((tops[chunk] - top) * factor)
        inverse = 1.0 / (sums[chunk] * shrink + jnp.sum(before + outer, axis=0, keepdims=True))
        before = before * inverse
        outer = outer * inverse
        middle = probs[OWN * tokens:(OWN + 1) * tokens, at] * (inverse * shrink)
        for number, part in enumerate((before, middle, outer)):
            probs[number * tokens:(number + 1) * tokens, at] = part
        for slot, part in enumerate((before, middle, jnp.where(back, outer, 0.0), jnp.where(back, 0.0, outer))):
            probs_half[slot * tokens:(slot + 1) * tokens, at] = part.astype(jnp.bfloat16)

    def store_parts(which, total):
        for number, (_, slot) in enumerate(halo):
            part_out[which, number] = total[slot * tokens:(slot + 1) * tokens].astype(jnp.bfloat16)
        own[which] = total[OWN * tokens:(OWN + 1) * tokens]

    def send_parts(which):
        each_halo(-1, lambda number: part_copy(which, number).start())

    local[4].wait()
    each_halo(-1, lambda number: halo_copy(1, number).wait_recv())
    for k in range(n_kvh):
        pltpu.make_async_copy(cot.at[k], cot.at[k], cot_recv.at[k]).wait()
    for k in range(n_kvh):
        block = cot[k].astype(jnp.float32).reshape(piece, -1)
        c2[pl.ds(k * piece, piece), :] = block.astype(jnp.bfloat16)

    order = (2, 1, 3, 0)
    v_all = vbuf[...].reshape(TILES * tokens, -1)
    k_turned = jnp.transpose(k_all.astype(jnp.float32)).astype(jnp.bfloat16)

    def chunk_of(step):
        target = lax.rem(chip + order[step], chips)
        return target, pl.ds(pl.multiple_of(target * width, width), width)

    def score_gradients(step):
        target, at = chunk_of(step)
        back = is_back(target)
        dprobs = lax.dot_general(v_all, c2[at, :], NT, preferred_element_type=jnp.float32)
        inner = dprobs[:2 * tokens]
        outer = jnp.where(back, dprobs[2 * tokens:3 * tokens], dprobs[3 * tokens:])
        inner_probs = probs[:2 * tokens, at]
        outer_probs = probs[2 * tokens:, at]
        delta = jnp.sum(inner_probs * inner, axis=0, keepdims=True)
        delta = delta + jnp.sum(outer_probs * outer, axis=0, keepdims=True)
        inner = (inner_probs * (inner - delta)).astype(jnp.bfloat16)
        outer = outer_probs * (outer - delta)
        far = jnp.where(back, outer, 0.0).astype(jnp.bfloat16)
        ahead = jnp.where(back, 0.0, outer).astype(jnp.bfloat16)
        return jnp.concatenate([inner, far, ahead], axis=0)

    def query_gradients(step, ds_chunk):
        target, _ = chunk_of(step)
        turned = jnp.dot(k_turned, ds_chunk, preferred_element_type=jnp.float32)
        block = (jnp.transpose(turned) * scale).reshape(2, piece // GROUP, GROUP, -1)
        gqbuf[pl.ds(2 * target, 2)] = block.astype(jnp.bfloat16)

    def key_gradients(step, ds_chunk):
        _, at = chunk_of(step)
        return jnp.dot(ds_chunk, q2[at, :], preferred_element_type=jnp.float32)

    queries = []

    def send_queries(step):
        target, _ = chunk_of(step)
        holders = [2 * target, 2 * target + 1] if order[step] else [partner]
        if not order[step]:
            pltpu.make_async_copy(gqbuf.at[me], gq_out.at[:, me], gq_recv.at[me]).start()
        for core, holder in enumerate(holders):
            copy = pltpu.make_async_remote_copy(
                gqbuf.at[holder], gq_out.at[:, me], gq_send.at[2 * step + core], gq_recv.at[me],
                device_id=(seq, holder), device_id_type=MESH,
            )
            copy.start()
            queries.append(copy)

    ds_chunk = score_gradients(0)
    store_parts(0, jnp.dot(probs_half[...], c2[...], preferred_element_type=jnp.float32))
    send_parts(0)
    key_total = None
    for step in range(chips):
        later = score_gradients(step + 1) if step + 1 < chips else None
        query_gradients(step, ds_chunk)
        term = key_gradients(step, ds_chunk)
        key_total = term if key_total is None else key_total + term
        if later is None:
            store_parts(1, key_total * scale)
            send_parts(1)
        send_queries(step)
        ds_chunk = later

    outs = []
    for which, out in ((0, gv_out), (1, gk_out)):
        total = own[which]
        each_halo(1, lambda number: part_copy(which, number).wait_recv())
        for number in range(3):
            total = total + part_in[which, number].astype(jnp.float32)
        final[which] = total.astype(jnp.bfloat16)
        copy = pltpu.make_async_copy(final.at[which], out, out_sem.at[which])
        copy.start()
        outs.append(copy)
    for k in range(n_kvh):
        pltpu.make_async_copy(gqbuf.at[k], gq_out.at[:, k], gq_recv.at[k]).wait()
    for which in (0, 1):
        each_halo(1, lambda number: halo_copy(which, number).wait_send())
        each_halo(-1, lambda number: part_copy(which, number).wait_send())
    for copy in sends + queries:
        copy.wait_send()
    for copy in outs:
        copy.wait()


def finish(gq_in, gk_in, gv_in, gq_out, gk_out, gv_out, sem):
    copies = [
        pltpu.make_async_copy(source, target, sem.at[number])
        for number, (source, target) in enumerate(((gq_in, gq_out), (gk_in, gk_out), (gv_in, gv_out)))
    ]
    for copy in copies:
        copy.start()
    for copy in copies:
        copy.wait()


def solution(mesh):
    n_seq, n_kvh = mesh.shape["seq"], mesh.shape["kvh"]

    def step(queries, keys, values, output_gradient, doc_lengths, prefix_lengths):
        tokens, heads, size = queries.shape
        mine = output_gradient.shape[0]
        rows = tokens * heads
        bf16, f32, docs = jnp.bfloat16, jnp.float32, doc_lengths.shape[0]
        anywhere = pl.BlockSpec(memory_space=pl.ANY)
        dma = pltpu.SemaphoreType.DMA
        shapes = (
            jax.ShapeDtypeStruct((mine, n_kvh, heads, size), bf16),
            jax.ShapeDtypeStruct((tokens, size), bf16),
            jax.ShapeDtypeStruct((tokens, size), bf16),
        )
        results = pl.pallas_call(
            functools.partial(kernel, n_seq, n_kvh, size ** -0.5),
            out_shape=shapes,
            in_specs=[pl.BlockSpec(memory_space=pltpu.HBM)] * 6,
            out_specs=(anywhere,) * 3,
            scratch_shapes=[
                pltpu.VMEM((tokens, heads, size), bf16),
                pltpu.VMEM((TILES, tokens, size), bf16),
                pltpu.VMEM((TILES, tokens, size), bf16),
                pltpu.VMEM((n_kvh, mine, heads, size), bf16),
                pltpu.VMEM((1, docs), jnp.int32),
                pltpu.VMEM((1, docs), jnp.int32),
                pltpu.VMEM((rows, size), bf16),
                pltpu.VMEM((rows, size), bf16),
                pltpu.VMEM(((TILES - 1) * tokens, rows), f32),
                pltpu.VMEM((TILES * tokens, rows), bf16),
                pltpu.VMEM((n_kvh, mine, heads, size), bf16),
                pltpu.VMEM((2, 3, tokens, size), bf16),
                pltpu.VMEM((2, 3, tokens, size), bf16),
                pltpu.VMEM((2, tokens, size), f32),
                pltpu.VMEM((2, tokens, size), bf16),
                dma((5,)),
                dma((2, 3)),
                dma((2, 3)),
                dma((n_kvh,)),
                dma((n_kvh,)),
                dma((n_kvh,)),
                dma((n_kvh,)),
                dma((2, 3)),
                dma((2, 3)),
                dma((2,)),
                pltpu.SemaphoreType.REGULAR,
            ],
            compiler_params=pltpu.CompilerParams(collective_id=0, has_side_effects=True, vmem_limit_bytes=VMEM_LIMIT),
        )(*(pltpu.with_memory_space_constraint(x, pltpu.HBM) for x in (
            queries,
            keys.reshape(tokens, size),
            values.reshape(tokens, size),
            output_gradient.reshape(mine, n_kvh, heads, size),
            doc_lengths.reshape(1, docs),
            prefix_lengths.reshape(1, docs),
        )))
        gq, gk, gv = pl.pallas_call(
            finish,
            out_shape=shapes,
            in_specs=[anywhere] * 3,
            out_specs=(pl.BlockSpec(memory_space=pltpu.HBM),) * 3,
            scratch_shapes=[dma((3,))],
            compiler_params=pltpu.CompilerParams(vmem_limit_bytes=1 << 20),
        )(*results)
        return gq.reshape(mine, n_kvh * heads, size), gk.reshape(tokens, 1, size), gv.reshape(tokens, 1, size)

    return jax.shard_map(
        step,
        mesh=mesh,
        in_specs=(P("seq", "kvh", None),) * 3 + (P(("seq", "kvh"), None, None), P(), P()),
        out_specs=(P(("seq", "kvh"), None, None), P("seq", "kvh", None), P("seq", "kvh", None)),
        check_vma=False,
    )
```

```python
import functools

import jax
import jax.numpy as jnp
from jax import lax
from jax.experimental import pallas as pl
from jax.experimental.pallas import tpu as pltpu
from jax.sharding import PartitionSpec as P

MESH = pl.DeviceIdType.MESH
GROUP = 8
TILES = 4
OWN = 1
VMEM_LIMIT = 32 << 20
LOG2E = 1.4426950408889634
NT = (((1,), (1,)), ((), ()))


def key_interval(positions, doc_len, doc_prefix, doc_start):
    start = jnp.max(jnp.where(doc_start <= positions, doc_start, 0), axis=0, keepdims=True)
    mine = doc_start == start
    length = jnp.sum(jnp.where(mine, doc_len, 0), axis=0, keepdims=True)
    prefix = jnp.sum(jnp.where(mine, doc_prefix, 0), axis=0, keepdims=True)
    stop = jnp.minimum(start + length, jnp.maximum(positions + 1, start + prefix))
    return start, stop


def kernel(
    n_seq, n_kvh, scale,
    q_hbm, k_hbm, v_hbm, og_hbm, len_hbm, pre_hbm,
    gq_out, gk_out, gv_out,
    qbuf, kbuf, vbuf, cot, lens, pres, q2, c2, probs, probs_half, gqbuf,
    part_out, part_in, own, final,
    local_sem, kv_send, kv_recv, cot_send, cot_recv, gq_send, gq_recv, part_send, part_recv, out_sem, ready,
):
    seq = lax.axis_index("seq")
    me = lax.axis_index("kvh")
    chip = me // 2
    chips = n_kvh // 2
    partner = me + 1 - 2 * lax.rem(me, 2)
    rows = q2.shape[0]
    tokens = kbuf.shape[1]
    piece = rows // n_kvh
    width = 2 * piece

    def inside(distance):
        return (seq + distance >= 0) & (seq + distance < n_seq)

    barrier = pltpu.get_barrier_semaphore()
    for d in range(1, n_kvh):
        other = (seq, lax.rem(me + d, n_kvh))
        pl.semaphore_signal(barrier, inc=1, device_id=other, device_id_type=MESH)
    for d in (-2, -1):
        @pl.when(inside(d))
        def _(d=d):
            pl.semaphore_signal(barrier, inc=1, device_id=(seq + d, me), device_id_type=MESH)

    local = [
        pltpu.make_async_copy(len_hbm, lens, local_sem.at[0]),
        pltpu.make_async_copy(pre_hbm, pres, local_sem.at[1]),
        pltpu.make_async_copy(q_hbm, qbuf, local_sem.at[2]),
        pltpu.make_async_copy(k_hbm, kbuf.at[OWN], local_sem.at[3]),
        pltpu.make_async_copy(v_hbm, vbuf.at[OWN], local_sem.at[4]),
        pltpu.make_async_copy(og_hbm.at[:, me], cot.at[me], cot_recv.at[me]),
    ]
    for copy in local:
        copy.start()
    halo = ((2, 2), (1, 0), (-1, 3))
    for number, (distance, slot) in enumerate(halo):
        @pl.when(jnp.logical_not(inside(-distance)))
        def _(slot=slot):
            kbuf[slot] = jnp.zeros_like(kbuf[slot])
            vbuf[slot] = jnp.zeros_like(vbuf[slot])

        @pl.when(jnp.logical_not(inside(distance)))
        def _(number=number):
            part_in[:, number] = jnp.zeros_like(part_in[:, number])
    pl.semaphore_wait(barrier, n_kvh - 1 + sum(inside(d).astype(jnp.int32) for d in (1, 2)))

    def halo_copy(which, number):
        distance, slot = halo[number]
        source, target = ((k_hbm, kbuf), (v_hbm, vbuf))[which]
        return pltpu.make_async_remote_copy(
            source, target.at[slot], kv_send.at[which, number], kv_recv.at[which, number],
            device_id=(seq + distance, me), device_id_type=MESH,
        )

    def part_copy(which, number):
        distance, _ = halo[number]
        return pltpu.make_async_remote_copy(
            part_out.at[which, number], part_in.at[which, number],
            part_send.at[which, number], part_recv.at[which, number],
            device_id=(seq - distance, me), device_id_type=MESH,
        )

    def each_halo(sign, act):
        for number, (distance, _) in enumerate(halo):
            pl.when(inside(sign * distance))(functools.partial(act, number))

    @pl.when(inside(1))
    def _():
        pl.semaphore_signal(ready, inc=1, device_id=(seq + 1, me), device_id_type=MESH)
    for number in (0, 1):
        pl.when(inside(halo[number][0]))(lambda number=number: halo_copy(0, number).start())
    sends = []
    targets = [2 * lax.rem(chip + d, chips) + core for d in (2, 1, 3) for core in (0, 1)]
    targets.append(partner)
    for number, target in enumerate(targets):
        copy = pltpu.make_async_remote_copy(
            og_hbm.at[:, target], cot.at[me], cot_send.at[number], cot_recv.at[me],
            device_id=(seq, target), device_id_type=MESH,
        )
        copy.start()
        sends.append(copy)
    for number in (0, 1):
        pl.when(inside(halo[number][0]))(lambda number=number: halo_copy(1, number).start())

    @pl.when(inside(-1))
    def _():
        pl.semaphore_wait(ready, 1)
        halo_copy(0, 2).start()
        halo_copy(1, 2).start()

    local[0].wait()
    local[1].wait()
    docs = lens.shape[1]
    square = (docs, docs)
    by_sublane = lax.broadcasted_iota(jnp.int32, square, 0)
    by_lane = lax.broadcasted_iota(jnp.int32, square, 1)
    doc_len = jnp.transpose(jnp.broadcast_to(lens[...], square))
    doc_prefix = jnp.transpose(jnp.broadcast_to(pres[...], square))
    start_row = jnp.sum(jnp.where(by_sublane < by_lane, doc_len, 0), axis=0, keepdims=True)
    doc_start = jnp.transpose(jnp.broadcast_to(start_row, square))
    bounds = []
    for block in range(rows // docs):
        positions = seq * tokens + block * (docs // GROUP) + (by_lane[:1] >> 3)
        bounds.append(key_interval(positions, doc_len, doc_prefix, doc_start))

    tile = (tokens, width)
    key_at = lax.broadcasted_iota(jnp.int32, tile, 0)
    token_at = lax.broadcasted_iota(jnp.int32, tile, 1) >> 3
    factor = scale * LOG2E

    def is_back(chunk):
        return key_at > token_at + chunk * (width // GROUP)

    def hidden(scores, positions, bound):
        return jnp.where((positions >= bound[0]) & (positions < bound[1]), scores, -1e30)

    local[2].wait()
    local[3].wait()
    per_chunk = width // docs
    limits, tops, sums = [], [], []
    for chunk in range(chips):
        at = pl.ds(chunk * width, width)
        block = qbuf[pl.ds(chunk * (width // GROUP), width // GROUP)].astype(jnp.float32)
        q_chunk = block.reshape(width, -1).astype(jnp.bfloat16)
        q2[at, :] = q_chunk
        limits.append([
            jnp.concatenate([b[side] for b in bounds[chunk * per_chunk:(chunk + 1) * per_chunk]], axis=1)
            for side in (0, 1)
        ])
        scores = lax.dot_general(kbuf[OWN], q_chunk, NT, preferred_element_type=jnp.float32)
        scores = hidden(scores, key_at + seq * tokens, limits[chunk])
        tops.append(jnp.max(scores, axis=0, keepdims=True))
        expo = jnp.exp2((scores - tops[chunk]) * factor)
        sums.append(jnp.sum(expo, axis=0, keepdims=True))
        probs[OWN * tokens:(OWN + 1) * tokens, at] = expo

    for number in (0, 1, 2):
        pl.when(inside(-halo[number][0]))(lambda number=number: halo_copy(0, number).wait_recv())
    k_all = kbuf[...].reshape(TILES * tokens, -1)
    for chunk in range(chips):
        at = pl.ds(chunk * width, width)
        back = is_back(chunk)
        before, _, far, ahead = (
            lax.dot_general(kbuf[slot], q2[at, :], NT, preferred_element_type=jnp.float32) if slot != OWN else None
            for slot in range(TILES)
        )
        before = hidden(before, key_at + (seq - 1) * tokens, limits[chunk])
        outer = hidden(
            jnp.where(back, far, ahead),
            key_at + jnp.where(back, (seq - 2) * tokens, (seq + 1) * tokens),
            limits[chunk],
        )
        top = jnp.maximum(tops[chunk], jnp.max(jnp.maximum(before, outer), axis=0, keepdims=True))
        before = jnp.exp2((before - top) * factor)
        outer = jnp.exp2((outer - top) * factor)
        shrink = jnp.exp2((tops[chunk] - top) * factor)
        inverse = 1.0 / (sums[chunk] * shrink + jnp.sum(before + outer, axis=0, keepdims=True))
        before = before * inverse
        outer = outer * inverse
        middle = probs[OWN * tokens:(OWN + 1) * tokens, at] * (inverse * shrink)
        for number, part in enumerate((before, middle, outer)):
            probs[number * tokens:(number + 1) * tokens, at] = part
        for slot, part in enumerate((before, middle, jnp.where(back, outer, 0.0), jnp.where(back, 0.0, outer))):
            probs_half[slot * tokens:(slot + 1) * tokens, at] = part.astype(jnp.bfloat16)

    def store_parts(which, total):
        for number, (_, slot) in enumerate(halo):
            part_out[which, number] = total[slot * tokens:(slot + 1) * tokens].astype(jnp.bfloat16)
        own[which] = total[OWN * tokens:(OWN + 1) * tokens]

    def send_parts(which):
        each_halo(-1, lambda number: part_copy(which, number).start())

    local[4].wait()
    each_halo(-1, lambda number: halo_copy(1, number).wait_recv())
    order = (0, 1, 3, 2)
    v_all = vbuf[...].reshape(TILES * tokens, -1)
    k_turned = jnp.transpose(k_all.astype(jnp.float32)).astype(jnp.bfloat16)

    def chunk_of(step):
        target = lax.rem(chip + order[step], chips)
        return target, pl.ds(pl.multiple_of(target * width, width), width)

    def cotangents(step):
        target, _ = chunk_of(step)
        for core in (0, 1):
            holder = 2 * target + core
            pltpu.make_async_copy(cot.at[holder], cot.at[holder], cot_recv.at[holder]).wait()
        for core in (0, 1):
            holder = 2 * target + core
            block = cot[holder].astype(jnp.float32).reshape(piece, -1)
            c2[pl.ds(pl.multiple_of(holder * piece, piece), piece), :] = block.astype(jnp.bfloat16)

    def score_gradients(step):
        target, at = chunk_of(step)
        back = is_back(target)
        dprobs = lax.dot_general(v_all, c2[at, :], NT, preferred_element_type=jnp.float32)
        inner = dprobs[:2 * tokens]
        outer = jnp.where(back, dprobs[2 * tokens:3 * tokens], dprobs[3 * tokens:])
        inner_probs = probs[:2 * tokens, at]
        outer_probs = probs[2 * tokens:, at]
        delta = jnp.sum(inner_probs * inner, axis=0, keepdims=True)
        delta = delta + jnp.sum(outer_probs * outer, axis=0, keepdims=True)
        inner = (inner_probs * (inner - delta)).astype(jnp.bfloat16)
        outer = outer_probs * (outer - delta)
        far = jnp.where(back, outer, 0.0).astype(jnp.bfloat16)
        ahead = jnp.where(back, 0.0, outer).astype(jnp.bfloat16)
        return jnp.concatenate([inner, far, ahead], axis=0)

    def query_gradients(step, ds_chunk):
        target, _ = chunk_of(step)
        turned = jnp.dot(k_turned, ds_chunk, preferred_element_type=jnp.float32)
        block = (jnp.transpose(turned) * scale).reshape(2, piece // GROUP, GROUP, -1)
        gqbuf[pl.ds(2 * target, 2)] = block.astype(jnp.bfloat16)

    def key_gradients(step, ds_chunk):
        _, at = chunk_of(step)
        return jnp.dot(ds_chunk, q2[at, :], preferred_element_type=jnp.float32)

    queries = []

    def send_queries(step):
        target, _ = chunk_of(step)
        holders = [2 * target, 2 * target + 1] if order[step] else [partner]
        if not order[step]:
            pltpu.make_async_copy(gqbuf.at[me], gq_out.at[:, me], gq_recv.at[me]).start()
        for core, holder in enumerate(holders):
            copy = pltpu.make_async_remote_copy(
                gqbuf.at[holder], gq_out.at[:, me], gq_send.at[2 * step + core], gq_recv.at[me],
                device_id=(seq, holder), device_id_type=MESH,
            )
            copy.start()
            queries.append(copy)

    cotangents(0)
    ds_chunk = score_gradients(0)
    query_gradients(0, ds_chunk)
    key_total = key_gradients(0, ds_chunk)
    send_queries(0)
    cotangents(1)
    ds_chunk = score_gradients(1)
    for step in range(1, chips):
        later = None
        if step + 1 < chips:
            cotangents(step + 1)
            if step + 2 == chips:
                store_parts(0, jnp.dot(probs_half[...], c2[...], preferred_element_type=jnp.float32))
                send_parts(0)
            later = score_gradients(step + 1)
        query_gradients(step, ds_chunk)
        key_total = key_total + key_gradients(step, ds_chunk)
        if later is None:
            store_parts(1, key_total * scale)
            send_parts(1)
        send_queries(step)
        ds_chunk = later

    outs = []
    for which, out in ((0, gv_out), (1, gk_out)):
        total = own[which]
        each_halo(1, lambda number: part_copy(which, number).wait_recv())
        for number in range(3):
            total = total + part_in[which, number].astype(jnp.float32)
        final[which] = total.astype(jnp.bfloat16)
        copy = pltpu.make_async_copy(final.at[which], out, out_sem.at[which])
        copy.start()
        outs.append(copy)
    for k in range(n_kvh):
        pltpu.make_async_copy(gqbuf.at[k], gq_out.at[:, k], gq_recv.at[k]).wait()
    for which in (0, 1):
        each_halo(1, lambda number: halo_copy(which, number).wait_send())
        each_halo(-1, lambda number: part_copy(which, number).wait_send())
    for copy in sends + queries:
        copy.wait_send()
    for copy in outs:
        copy.wait()


def finish(gq_in, gk_in, gv_in, gq_out, gk_out, gv_out, sem):
    copies = [
        pltpu.make_async_copy(source, target, sem.at[number])
        for number, (source, target) in enumerate(((gq_in, gq_out), (gk_in, gk_out), (gv_in, gv_out)))
    ]
    for copy in copies:
        copy.start()
    for copy in copies:
        copy.wait()


def solution(mesh):
    n_seq, n_kvh = mesh.shape["seq"], mesh.shape["kvh"]

    def step(queries, keys, values, output_gradient, doc_lengths, prefix_lengths):
        tokens, heads, size = queries.shape
        mine = output_gradient.shape[0]
        rows = tokens * heads
        bf16, f32, docs = jnp.bfloat16, jnp.float32, doc_lengths.shape[0]
        anywhere = pl.BlockSpec(memory_space=pl.ANY)
        dma = pltpu.SemaphoreType.DMA
        shapes = (
            jax.ShapeDtypeStruct((mine, n_kvh, heads, size), bf16),
            jax.ShapeDtypeStruct((tokens, size), bf16),
            jax.ShapeDtypeStruct((tokens, size), bf16),
        )
        results = pl.pallas_call(
            functools.partial(kernel, n_seq, n_kvh, size ** -0.5),
            out_shape=shapes,
            in_specs=[pl.BlockSpec(memory_space=pltpu.HBM)] * 6,
            out_specs=(anywhere,) * 3,
            scratch_shapes=[
                pltpu.VMEM((tokens, heads, size), bf16),
                pltpu.VMEM((TILES, tokens, size), bf16),
                pltpu.VMEM((TILES, tokens, size), bf16),
                pltpu.VMEM((n_kvh, mine, heads, size), bf16),
                pltpu.VMEM((1, docs), jnp.int32),
                pltpu.VMEM((1, docs), jnp.int32),
                pltpu.VMEM((rows, size), bf16),
                pltpu.VMEM((rows, size), bf16),
                pltpu.VMEM(((TILES - 1) * tokens, rows), f32),
                pltpu.VMEM((TILES * tokens, rows), bf16),
                pltpu.VMEM((n_kvh, mine, heads, size), bf16),
                pltpu.VMEM((2, 3, tokens, size), bf16),
                pltpu.VMEM((2, 3, tokens, size), bf16),
                pltpu.VMEM((2, tokens, size), f32),
                pltpu.VMEM((2, tokens, size), bf16),
                dma((5,)),
                dma((2, 3)),
                dma((2, 3)),
                dma((n_kvh,)),
                dma((n_kvh,)),
                dma((n_kvh,)),
                dma((n_kvh,)),
                dma((2, 3)),
                dma((2, 3)),
                dma((2,)),
                pltpu.SemaphoreType.REGULAR,
            ],
            compiler_params=pltpu.CompilerParams(collective_id=0, has_side_effects=True, vmem_limit_bytes=VMEM_LIMIT),
        )(*(pltpu.with_memory_space_constraint(x, pltpu.HBM) for x in (
            queries,
            keys.reshape(tokens, size),
            values.reshape(tokens, size),
            output_gradient.reshape(mine, n_kvh, heads, size),
            doc_lengths.reshape(1, docs),
            prefix_lengths.reshape(1, docs),
        )))
        gq, gk, gv = pl.pallas_call(
            finish,
            out_shape=shapes,
            in_specs=[anywhere] * 3,
            out_specs=(pl.BlockSpec(memory_space=pltpu.HBM),) * 3,
            scratch_shapes=[dma((3,))],
            compiler_params=pltpu.CompilerParams(vmem_limit_bytes=1 << 20),
        )(*results)
        return gq.reshape(mine, n_kvh * heads, size), gk.reshape(tokens, 1, size), gv.reshape(tokens, 1, size)

    return jax.shard_map(
        step,
        mesh=mesh,
        in_specs=(P("seq", "kvh", None),) * 3 + (P(("seq", "kvh"), None, None), P(), P()),
        out_specs=(P(("seq", "kvh"), None, None), P("seq", "kvh", None), P("seq", "kvh", None)),
        check_vma=False,
    )
```

```python
import functools

import jax
import jax.numpy as jnp
from jax import lax
from jax.experimental import pallas as pl
from jax.experimental.pallas import tpu as pltpu
from jax.sharding import PartitionSpec as P

MESH = pl.DeviceIdType.MESH
GROUP = 8
TILES = 4
OWN = 1
VMEM_LIMIT = 32 << 20
LOG2E = 1.4426950408889634
NT = (((1,), (1,)), ((), ()))


def key_interval(positions, doc_len, doc_prefix, doc_start):
    start = jnp.max(jnp.where(doc_start <= positions, doc_start, 0), axis=0, keepdims=True)
    mine = doc_start == start
    length = jnp.sum(jnp.where(mine, doc_len, 0), axis=0, keepdims=True)
    prefix = jnp.sum(jnp.where(mine, doc_prefix, 0), axis=0, keepdims=True)
    stop = jnp.minimum(start + length, jnp.maximum(positions + 1, start + prefix))
    return start, stop


def kernel(
    n_seq, n_kvh, scale,
    q_hbm, k_hbm, v_hbm, og_hbm, len_hbm, pre_hbm,
    gq_out, gk_out, gv_out,
    qbuf, kbuf, vbuf, cot, lens, pres, q2, c2, probs, probs_half, gqbuf,
    part_out, part_in, own, final,
    local_sem, kv_send, kv_recv, cot_send, cot_recv, gq_send, gq_recv, part_send, part_recv, out_sem, ready,
):
    seq = lax.axis_index("seq")
    me = lax.axis_index("kvh")
    chip = me // 2
    chips = n_kvh // 2
    partner = me + 1 - 2 * lax.rem(me, 2)
    rows = q2.shape[0]
    tokens = kbuf.shape[1]
    piece = rows // n_kvh
    width = 2 * piece

    def inside(distance):
        return (seq + distance >= 0) & (seq + distance < n_seq)

    barrier = pltpu.get_barrier_semaphore()
    for d in range(1, n_kvh):
        other = (seq, lax.rem(me + d, n_kvh))
        pl.semaphore_signal(barrier, inc=1, device_id=other, device_id_type=MESH)
    for d in (-2, -1):
        @pl.when(inside(d))
        def _(d=d):
            pl.semaphore_signal(barrier, inc=1, device_id=(seq + d, me), device_id_type=MESH)

    local = [
        pltpu.make_async_copy(len_hbm, lens, local_sem.at[0]),
        pltpu.make_async_copy(pre_hbm, pres, local_sem.at[1]),
        pltpu.make_async_copy(q_hbm, qbuf, local_sem.at[2]),
        pltpu.make_async_copy(k_hbm, kbuf.at[OWN], local_sem.at[3]),
        pltpu.make_async_copy(v_hbm, vbuf.at[OWN], local_sem.at[4]),
        pltpu.make_async_copy(og_hbm.at[:, me], cot.at[me], cot_recv.at[me]),
    ]
    for copy in local:
        copy.start()
    halo = ((2, 2), (1, 0), (-1, 3))
    for number, (distance, slot) in enumerate(halo):
        @pl.when(jnp.logical_not(inside(-distance)))
        def _(slot=slot):
            kbuf[slot] = jnp.zeros_like(kbuf[slot])
            vbuf[slot] = jnp.zeros_like(vbuf[slot])

        @pl.when(jnp.logical_not(inside(distance)))
        def _(number=number):
            part_in[:, number] = jnp.zeros_like(part_in[:, number])
    pl.semaphore_wait(barrier, n_kvh - 1 + sum(inside(d).astype(jnp.int32) for d in (1, 2)))

    def halo_copy(which, number):
        distance, slot = halo[number]
        source, target = ((k_hbm, kbuf), (v_hbm, vbuf))[which]
        return pltpu.make_async_remote_copy(
            source, target.at[slot], kv_send.at[which, number], kv_recv.at[which, number],
            device_id=(seq + distance, me), device_id_type=MESH,
        )

    def part_copy(which, number):
        distance, _ = halo[number]
        return pltpu.make_async_remote_copy(
            part_out.at[which, number], part_in.at[which, number],
            part_send.at[which, number], part_recv.at[which, number],
            device_id=(seq - distance, me), device_id_type=MESH,
        )

    def each_halo(sign, act):
        for number, (distance, _) in enumerate(halo):
            pl.when(inside(sign * distance))(functools.partial(act, number))

    @pl.when(inside(1))
    def _():
        pl.semaphore_signal(ready, inc=1, device_id=(seq + 1, me), device_id_type=MESH)
    for number in (0, 1):
        pl.when(inside(halo[number][0]))(lambda number=number: halo_copy(0, number).start())
    sends = []
    targets = [2 * lax.rem(chip + d, chips) + core for d in (2, 1, 3) for core in (0, 1)]
    targets.append(partner)
    for number, target in enumerate(targets):
        copy = pltpu.make_async_remote_copy(
            og_hbm.at[:, target], cot.at[me], cot_send.at[number], cot_recv.at[me],
            device_id=(seq, target), device_id_type=MESH,
        )
        copy.start()
        sends.append(copy)
    for number in (0, 1):
        pl.when(inside(halo[number][0]))(lambda number=number: halo_copy(1, number).start())

    @pl.when(inside(-1))
    def _():
        pl.semaphore_wait(ready, 1)
        halo_copy(0, 2).start()
        halo_copy(1, 2).start()

    local[0].wait()
    local[1].wait()
    docs = lens.shape[1]
    square = (docs, docs)
    by_sublane = lax.broadcasted_iota(jnp.int32, square, 0)
    by_lane = lax.broadcasted_iota(jnp.int32, square, 1)
    doc_len = jnp.transpose(jnp.broadcast_to(lens[...], square))
    doc_prefix = jnp.transpose(jnp.broadcast_to(pres[...], square))
    start_row = jnp.sum(jnp.where(by_sublane < by_lane, doc_len, 0), axis=0, keepdims=True)
    doc_start = jnp.transpose(jnp.broadcast_to(start_row, square))
    bounds = []
    for block in range(rows // docs):
        positions = seq * tokens + block * (docs // GROUP) + (by_lane[:1] >> 3)
        bounds.append(key_interval(positions, doc_len, doc_prefix, doc_start))

    tile = (tokens, width)
    key_at = lax.broadcasted_iota(jnp.int32, tile, 0)
    token_at = lax.broadcasted_iota(jnp.int32, tile, 1) >> 3
    factor = scale * LOG2E

    def is_back(chunk):
        return key_at > token_at + chunk * (width // GROUP)

    def hidden(scores, positions, bound):
        return jnp.where((positions >= bound[0]) & (positions < bound[1]), scores, -1e30)

    local[2].wait()
    local[3].wait()
    per_chunk = width // docs
    limits, tops, sums = [], [], []
    for chunk in range(chips):
        at = pl.ds(chunk * width, width)
        block = qbuf[pl.ds(chunk * (width // GROUP), width // GROUP)].astype(jnp.float32)
        q_chunk = block.reshape(width, -1).astype(jnp.bfloat16)
        q2[at, :] = q_chunk
        limits.append([
            jnp.concatenate([b[side] for b in bounds[chunk * per_chunk:(chunk + 1) * per_chunk]], axis=1)
            for side in (0, 1)
        ])
        scores = lax.dot_general(kbuf[OWN], q_chunk, NT, preferred_element_type=jnp.float32)
        scores = hidden(scores, key_at + seq * tokens, limits[chunk])
        tops.append(jnp.max(scores, axis=0, keepdims=True))
        expo = jnp.exp2((scores - tops[chunk]) * factor)
        sums.append(jnp.sum(expo, axis=0, keepdims=True))
        probs[OWN * tokens:(OWN + 1) * tokens, at] = expo

    for number in (0, 1, 2):
        pl.when(inside(-halo[number][0]))(lambda number=number: halo_copy(0, number).wait_recv())
    k_all = kbuf[...].reshape(TILES * tokens, -1)
    for chunk in range(chips):
        at = pl.ds(chunk * width, width)
        back = is_back(chunk)
        before, _, far, ahead = (
            lax.dot_general(kbuf[slot], q2[at, :], NT, preferred_element_type=jnp.float32) if slot != OWN else None
            for slot in range(TILES)
        )
        before = hidden(before, key_at + (seq - 1) * tokens, limits[chunk])
        outer = hidden(
            jnp.where(back, far, ahead),
            key_at + jnp.where(back, (seq - 2) * tokens, (seq + 1) * tokens),
            limits[chunk],
        )
        top = jnp.maximum(tops[chunk], jnp.max(jnp.maximum(before, outer), axis=0, keepdims=True))
        before = jnp.exp2((before - top) * factor)
        outer = jnp.exp2((outer - top) * factor)
        shrink = jnp.exp2((tops[chunk] - top) * factor)
        inverse = 1.0 / (sums[chunk] * shrink + jnp.sum(before + outer, axis=0, keepdims=True))
        before = before * inverse
        outer = outer * inverse
        middle = probs[OWN * tokens:(OWN + 1) * tokens, at] * (inverse * shrink)
        for number, part in enumerate((before, middle, outer)):
            probs[number * tokens:(number + 1) * tokens, at] = part
        for slot, part in enumerate((before, middle, jnp.where(back, outer, 0.0), jnp.where(back, 0.0, outer))):
            probs_half[slot * tokens:(slot + 1) * tokens, at] = part.astype(jnp.bfloat16)

    def store_parts(which, total):
        for number, (_, slot) in enumerate(halo):
            part_out[which, number] = total[slot * tokens:(slot + 1) * tokens].astype(jnp.bfloat16)
        own[which] = total[OWN * tokens:(OWN + 1) * tokens]

    def send_parts(which):
        each_halo(-1, lambda number: part_copy(which, number).start())

    local[4].wait()
    each_halo(-1, lambda number: halo_copy(1, number).wait_recv())
    for k in range(n_kvh):
        pltpu.make_async_copy(cot.at[k], cot.at[k], cot_recv.at[k]).wait()
    for k in range(n_kvh):
        block = cot[k].astype(jnp.float32).reshape(piece, -1)
        c2[pl.ds(k * piece, piece), :] = block.astype(jnp.bfloat16)

    order = (2, 1, 3, 0)
    v_all = vbuf[...].reshape(TILES * tokens, -1)
    k_turned = jnp.transpose(k_all.astype(jnp.float32)).astype(jnp.bfloat16)

    def chunk_of(step):
        target = lax.rem(chip + order[step], chips)
        return target, pl.ds(pl.multiple_of(target * width, width), width)

    def score_gradients(step):
        target, at = chunk_of(step)
        back = is_back(target)
        dprobs = lax.dot_general(v_all, c2[at, :], NT, preferred_element_type=jnp.float32)
        inner = dprobs[:2 * tokens]
        outer = jnp.where(back, dprobs[2 * tokens:3 * tokens], dprobs[3 * tokens:])
        inner_probs = probs[:2 * tokens, at]
        outer_probs = probs[2 * tokens:, at]
        delta = jnp.sum(inner_probs * inner, axis=0, keepdims=True)
        delta = delta + jnp.sum(outer_probs * outer, axis=0, keepdims=True)
        inner = (inner_probs * (inner - delta)).astype(jnp.bfloat16)
        outer = outer_probs * (outer - delta)
        far = jnp.where(back, outer, 0.0).astype(jnp.bfloat16)
        ahead = jnp.where(back, 0.0, outer).astype(jnp.bfloat16)
        return jnp.concatenate([inner, far, ahead], axis=0)

    def query_gradients(step, ds_chunk):
        target, _ = chunk_of(step)
        turned = jnp.dot(k_turned, ds_chunk, preferred_element_type=jnp.float32)
        block = (jnp.transpose(turned) * scale).reshape(2, piece // GROUP, GROUP, -1)
        gqbuf[pl.ds(2 * target, 2)] = block.astype(jnp.bfloat16)

    def key_gradients(step, ds_chunk):
        _, at = chunk_of(step)
        return jnp.dot(ds_chunk, q2[at, :], preferred_element_type=jnp.float32)

    queries = []

    def send_queries(step):
        target, _ = chunk_of(step)
        holders = [2 * target, 2 * target + 1] if order[step] else [partner]
        if not order[step]:
            pltpu.make_async_copy(gqbuf.at[me], gq_out.at[:, me], gq_recv.at[me]).start()
        for core, holder in enumerate(holders):
            copy = pltpu.make_async_remote_copy(
                gqbuf.at[holder], gq_out.at[:, me], gq_send.at[2 * step + core], gq_recv.at[me],
                device_id=(seq, holder), device_id_type=MESH,
            )
            copy.start()
            queries.append(copy)

    ds_chunk = score_gradients(0)
    key_total = None
    for step in range(chips):
        if step == 2:
            store_parts(0, jnp.dot(probs_half[...], c2[...], preferred_element_type=jnp.float32))
            send_parts(0)
        later = score_gradients(step + 1) if step + 1 < chips else None
        query_gradients(step, ds_chunk)
        term = key_gradients(step, ds_chunk)
        key_total = term if key_total is None else key_total + term
        if later is None:
            store_parts(1, key_total * scale)
            send_parts(1)
        send_queries(step)
        ds_chunk = later

    outs = []
    for which, out in ((0, gv_out), (1, gk_out)):
        total = own[which]
        each_halo(1, lambda number: part_copy(which, number).wait_recv())
        for number in range(3):
            total = total + part_in[which, number].astype(jnp.float32)
        final[which] = total.astype(jnp.bfloat16)
        copy = pltpu.make_async_copy(final.at[which], out, out_sem.at[which])
        copy.start()
        outs.append(copy)
    for k in range(n_kvh):
        pltpu.make_async_copy(gqbuf.at[k], gq_out.at[:, k], gq_recv.at[k]).wait()
    for which in (0, 1):
        each_halo(1, lambda number: halo_copy(which, number).wait_send())
        each_halo(-1, lambda number: part_copy(which, number).wait_send())
    for copy in sends + queries:
        copy.wait_send()
    for copy in outs:
        copy.wait()


def finish(gq_in, gk_in, gv_in, gq_out, gk_out, gv_out, sem):
    copies = [
        pltpu.make_async_copy(source, target, sem.at[number])
        for number, (source, target) in enumerate(((gq_in, gq_out), (gk_in, gk_out), (gv_in, gv_out)))
    ]
    for copy in copies:
        copy.start()
    for copy in copies:
        copy.wait()


def solution(mesh):
    n_seq, n_kvh = mesh.shape["seq"], mesh.shape["kvh"]

    def step(queries, keys, values, output_gradient, doc_lengths, prefix_lengths):
        tokens, heads, size = queries.shape
        mine = output_gradient.shape[0]
        rows = tokens * heads
        bf16, f32, docs = jnp.bfloat16, jnp.float32, doc_lengths.shape[0]
        anywhere = pl.BlockSpec(memory_space=pl.ANY)
        dma = pltpu.SemaphoreType.DMA
        shapes = (
            jax.ShapeDtypeStruct((mine, n_kvh, heads, size), bf16),
            jax.ShapeDtypeStruct((tokens, size), bf16),
            jax.ShapeDtypeStruct((tokens, size), bf16),
        )
        results = pl.pallas_call(
            functools.partial(kernel, n_seq, n_kvh, size ** -0.5),
            out_shape=shapes,
            in_specs=[pl.BlockSpec(memory_space=pltpu.HBM)] * 6,
            out_specs=(anywhere,) * 3,
            scratch_shapes=[
                pltpu.VMEM((tokens, heads, size), bf16),
                pltpu.VMEM((TILES, tokens, size), bf16),
                pltpu.VMEM((TILES, tokens, size), bf16),
                pltpu.VMEM((n_kvh, mine, heads, size), bf16),
                pltpu.VMEM((1, docs), jnp.int32),
                pltpu.VMEM((1, docs), jnp.int32),
                pltpu.VMEM((rows, size), bf16),
                pltpu.VMEM((rows, size), bf16),
                pltpu.VMEM(((TILES - 1) * tokens, rows), f32),
                pltpu.VMEM((TILES * tokens, rows), bf16),
                pltpu.VMEM((n_kvh, mine, heads, size), bf16),
                pltpu.VMEM((2, 3, tokens, size), bf16),
                pltpu.VMEM((2, 3, tokens, size), bf16),
                pltpu.VMEM((2, tokens, size), f32),
                pltpu.VMEM((2, tokens, size), bf16),
                dma((5,)),
                dma((2, 3)),
                dma((2, 3)),
                dma((n_kvh,)),
                dma((n_kvh,)),
                dma((n_kvh,)),
                dma((n_kvh,)),
                dma((2, 3)),
                dma((2, 3)),
                dma((2,)),
                pltpu.SemaphoreType.REGULAR,
            ],
            compiler_params=pltpu.CompilerParams(collective_id=0, has_side_effects=True, vmem_limit_bytes=VMEM_LIMIT),
        )(*(pltpu.with_memory_space_constraint(x, pltpu.HBM) for x in (
            queries,
            keys.reshape(tokens, size),
            values.reshape(tokens, size),
            output_gradient.reshape(mine, n_kvh, heads, size),
            doc_lengths.reshape(1, docs),
            prefix_lengths.reshape(1, docs),
        )))
        gq, gk, gv = pl.pallas_call(
            finish,
            out_shape=shapes,
            in_specs=[anywhere] * 3,
            out_specs=(pl.BlockSpec(memory_space=pltpu.HBM),) * 3,
            scratch_shapes=[dma((3,))],
            compiler_params=pltpu.CompilerParams(vmem_limit_bytes=1 << 20),
        )(*results)
        return gq.reshape(mine, n_kvh * heads, size), gk.reshape(tokens, 1, size), gv.reshape(tokens, 1, size)

    return jax.shard_map(
        step,
        mesh=mesh,
        in_specs=(P("seq", "kvh", None),) * 3 + (P(("seq", "kvh"), None, None), P(), P()),
        out_specs=(P(("seq", "kvh"), None, None), P("seq", "kvh", None), P("seq", "kvh", None)),
        check_vma=False,
    )
```

```python
import functools

import jax
import jax.numpy as jnp
from jax import lax
from jax.experimental import pallas as pl
from jax.experimental.pallas import tpu as pltpu
from jax.sharding import PartitionSpec as P

MESH = pl.DeviceIdType.MESH
GROUP = 8
TILES = 4
OWN = 1
VMEM_LIMIT = 32 << 20
LOG2E = 1.4426950408889634
NT = (((1,), (1,)), ((), ()))


def key_interval(positions, doc_len, doc_prefix, doc_start):
    start = jnp.max(jnp.where(doc_start <= positions, doc_start, 0), axis=0, keepdims=True)
    mine = doc_start == start
    length = jnp.sum(jnp.where(mine, doc_len, 0), axis=0, keepdims=True)
    prefix = jnp.sum(jnp.where(mine, doc_prefix, 0), axis=0, keepdims=True)
    stop = jnp.minimum(start + length, jnp.maximum(positions + 1, start + prefix))
    return start, stop


def kernel(
    n_seq, n_kvh, scale,
    q_hbm, k_hbm, v_hbm, og_hbm, len_hbm, pre_hbm,
    gq_out, gk_out, gv_out,
    qbuf, kbuf, vbuf, cot, lens, pres, q2, c2, probs, probs_half, gqbuf,
    part_out, part_in, own, final,
    local_sem, kv_send, kv_recv, cot_send, cot_recv, gq_send, gq_recv, part_send, part_recv, out_sem, ready,
):
    seq = lax.axis_index("seq")
    me = lax.axis_index("kvh")
    chip = me // 2
    chips = n_kvh // 2
    partner = me + 1 - 2 * lax.rem(me, 2)
    rows = q2.shape[0]
    tokens = kbuf.shape[1]
    piece = rows // n_kvh
    width = 2 * piece

    def inside(distance):
        return (seq + distance >= 0) & (seq + distance < n_seq)

    barrier = pltpu.get_barrier_semaphore()
    for d in range(1, n_kvh):
        other = (seq, lax.rem(me + d, n_kvh))
        pl.semaphore_signal(barrier, inc=1, device_id=other, device_id_type=MESH)
    for d in (-2, -1):
        @pl.when(inside(d))
        def _(d=d):
            pl.semaphore_signal(barrier, inc=1, device_id=(seq + d, me), device_id_type=MESH)

    local = [
        pltpu.make_async_copy(len_hbm, lens, local_sem.at[0]),
        pltpu.make_async_copy(pre_hbm, pres, local_sem.at[1]),
        pltpu.make_async_copy(q_hbm, qbuf, local_sem.at[2]),
        pltpu.make_async_copy(k_hbm, kbuf.at[OWN], local_sem.at[3]),
        pltpu.make_async_copy(v_hbm, vbuf.at[OWN], local_sem.at[4]),
        pltpu.make_async_copy(og_hbm.at[:, me], cot.at[me], cot_recv.at[me]),
    ]
    for copy in local:
        copy.start()
    halo = ((2, 2), (1, 0), (-1, 3))
    for number, (distance, slot) in enumerate(halo):
        @pl.when(jnp.logical_not(inside(-distance)))
        def _(slot=slot):
            kbuf[slot] = jnp.zeros_like(kbuf[slot])
            vbuf[slot] = jnp.zeros_like(vbuf[slot])

        @pl.when(jnp.logical_not(inside(distance)))
        def _(number=number):
            part_in[:, number] = jnp.zeros_like(part_in[:, number])
    pl.semaphore_wait(barrier, n_kvh - 1 + sum(inside(d).astype(jnp.int32) for d in (1, 2)))

    def halo_copy(which, number):
        distance, slot = halo[number]
        source, target = ((k_hbm, kbuf), (v_hbm, vbuf))[which]
        return pltpu.make_async_remote_copy(
            source, target.at[slot], kv_send.at[which, number], kv_recv.at[which, number],
            device_id=(seq + distance, me), device_id_type=MESH,
        )

    def part_copy(which, number):
        distance, _ = halo[number]
        return pltpu.make_async_remote_copy(
            part_out.at[which, number], part_in.at[which, number],
            part_send.at[which, number], part_recv.at[which, number],
            device_id=(seq - distance, me), device_id_type=MESH,
        )

    def each_halo(sign, act):
        for number, (distance, _) in enumerate(halo):
            pl.when(inside(sign * distance))(functools.partial(act, number))

    @pl.when(inside(1))
    def _():
        pl.semaphore_signal(ready, inc=1, device_id=(seq + 1, me), device_id_type=MESH)
    for number in (0, 1):
        pl.when(inside(halo[number][0]))(lambda number=number: halo_copy(0, number).start())
    sends = []
    targets = [2 * lax.rem(chip + d, chips) + core for d in (2, 1, 3) for core in (0, 1)]
    targets.append(partner)
    for number, target in enumerate(targets):
        copy = pltpu.make_async_remote_copy(
            og_hbm.at[:, target], cot.at[me], cot_send.at[number], cot_recv.at[me],
            device_id=(seq, target), device_id_type=MESH,
        )
        copy.start()
        sends.append(copy)
    for number in (0, 1):
        pl.when(inside(halo[number][0]))(lambda number=number: halo_copy(1, number).start())

    @pl.when(inside(-1))
    def _():
        pl.semaphore_wait(ready, 1)
        halo_copy(0, 2).start()
        halo_copy(1, 2).start()

    local[0].wait()
    local[1].wait()
    docs = lens.shape[1]
    square = (docs, docs)
    by_sublane = lax.broadcasted_iota(jnp.int32, square, 0)
    by_lane = lax.broadcasted_iota(jnp.int32, square, 1)
    doc_len = jnp.transpose(jnp.broadcast_to(lens[...], square))
    doc_prefix = jnp.transpose(jnp.broadcast_to(pres[...], square))
    start_row = jnp.sum(jnp.where(by_sublane < by_lane, doc_len, 0), axis=0, keepdims=True)
    doc_start = jnp.transpose(jnp.broadcast_to(start_row, square))
    bounds = []
    for block in range(rows // docs):
        positions = seq * tokens + block * (docs // GROUP) + (by_lane[:1] >> 3)
        bounds.append(key_interval(positions, doc_len, doc_prefix, doc_start))

    tile = (tokens, width)
    key_at = lax.broadcasted_iota(jnp.int32, tile, 0)
    token_at = lax.broadcasted_iota(jnp.int32, tile, 1) >> 3
    factor = scale * LOG2E

    def is_back(chunk):
        return key_at > token_at + chunk * (width // GROUP)

    def hidden(scores, positions, bound):
        return jnp.where((positions >= bound[0]) & (positions < bound[1]), scores, -1e30)

    local[2].wait()
    local[3].wait()
    per_chunk = width // docs
    limits, tops, sums = [], [], []
    for chunk in range(chips):
        at = pl.ds(chunk * width, width)
        block = qbuf[pl.ds(chunk * (width // GROUP), width // GROUP)].astype(jnp.float32)
        q_chunk = block.reshape(width, -1).astype(jnp.bfloat16)
        q2[at, :] = q_chunk
        limits.append([
            jnp.concatenate([b[side] for b in bounds[chunk * per_chunk:(chunk + 1) * per_chunk]], axis=1)
            for side in (0, 1)
        ])
        scores = lax.dot_general(kbuf[OWN], q_chunk, NT, preferred_element_type=jnp.float32)
        scores = hidden(scores, key_at + seq * tokens, limits[chunk])
        tops.append(jnp.max(scores, axis=0, keepdims=True))
        expo = jnp.exp2((scores - tops[chunk]) * factor)
        sums.append(jnp.sum(expo, axis=0, keepdims=True))
        probs[OWN * tokens:(OWN + 1) * tokens, at] = expo

    for number in (0, 1, 2):
        pl.when(inside(-halo[number][0]))(lambda number=number: halo_copy(0, number).wait_recv())
    k_all = kbuf[...].reshape(TILES * tokens, -1)
    for chunk in range(chips):
        at = pl.ds(chunk * width, width)
        back = is_back(chunk)
        before, _, far, ahead = (
            lax.dot_general(kbuf[slot], q2[at, :], NT, preferred_element_type=jnp.float32) if slot != OWN else None
            for slot in range(TILES)
        )
        before = hidden(before, key_at + (seq - 1) * tokens, limits[chunk])
        outer = hidden(
            jnp.where(back, far, ahead),
            key_at + jnp.where(back, (seq - 2) * tokens, (seq + 1) * tokens),
            limits[chunk],
        )
        top = jnp.maximum(tops[chunk], jnp.max(jnp.maximum(before, outer), axis=0, keepdims=True))
        before = jnp.exp2((before - top) * factor)
        outer = jnp.exp2((outer - top) * factor)
        shrink = jnp.exp2((tops[chunk] - top) * factor)
        inverse = 1.0 / (sums[chunk] * shrink + jnp.sum(before + outer, axis=0, keepdims=True))
        before = before * inverse
        outer = outer * inverse
        middle = probs[OWN * tokens:(OWN + 1) * tokens, at] * (inverse * shrink)
        for number, part in enumerate((before, middle, outer)):
            probs[number * tokens:(number + 1) * tokens, at] = part
        for slot, part in enumerate((before, middle, jnp.where(back, outer, 0.0), jnp.where(back, 0.0, outer))):
            probs_half[slot * tokens:(slot + 1) * tokens, at] = part.astype(jnp.bfloat16)

    def store_parts(which, before, outer):
        for number, part in ((1, before), (0, outer[:tokens]), (2, outer[tokens:])):
            part_out[which, number] = part.astype(jnp.bfloat16)

    def send_parts(which):
        each_halo(-1, lambda number: part_copy(which, number).start())

    local[4].wait()
    each_halo(-1, lambda number: halo_copy(1, number).wait_recv())
    for k in range(n_kvh):
        pltpu.make_async_copy(cot.at[k], cot.at[k], cot_recv.at[k]).wait()
    for k in range(n_kvh):
        block = cot[k].astype(jnp.float32).reshape(piece, -1)
        c2[pl.ds(k * piece, piece), :] = block.astype(jnp.bfloat16)

    order = (2, 1, 3, 0)
    v_all = vbuf[...].reshape(TILES * tokens, -1)
    k_turned = jnp.transpose(k_all.astype(jnp.float32)).astype(jnp.bfloat16)

    def chunk_of(step):
        target = lax.rem(chip + order[step], chips)
        return target, pl.ds(pl.multiple_of(target * width, width), width)

    def score_gradients(step):
        target, at = chunk_of(step)
        back = is_back(target)
        dprobs = lax.dot_general(v_all, c2[at, :], NT, preferred_element_type=jnp.float32)
        inner = dprobs[:2 * tokens]
        outer = jnp.where(back, dprobs[2 * tokens:3 * tokens], dprobs[3 * tokens:])
        inner_probs = probs[:2 * tokens, at]
        outer_probs = probs[2 * tokens:, at]
        delta = jnp.sum(inner_probs * inner, axis=0, keepdims=True)
        delta = delta + jnp.sum(outer_probs * outer, axis=0, keepdims=True)
        inner = (inner_probs * (inner - delta)).astype(jnp.bfloat16)
        outer = outer_probs * (outer - delta)
        far = jnp.where(back, outer, 0.0).astype(jnp.bfloat16)
        ahead = jnp.where(back, 0.0, outer).astype(jnp.bfloat16)
        return jnp.concatenate([inner, far, ahead], axis=0)

    def query_gradients(step, ds_chunk):
        target, _ = chunk_of(step)
        turned = jnp.dot(k_turned, ds_chunk, preferred_element_type=jnp.float32)
        block = (jnp.transpose(turned) * scale).reshape(2, piece // GROUP, GROUP, -1)
        gqbuf[pl.ds(2 * target, 2)] = block.astype(jnp.bfloat16)

    def key_gradients(step, ds_chunk):
        _, at = chunk_of(step)
        return jnp.dot(ds_chunk, q2[at, :], preferred_element_type=jnp.float32)

    queries = []

    def send_queries(step):
        target, _ = chunk_of(step)
        holders = [2 * target, 2 * target + 1] if order[step] else [partner]
        if not order[step]:
            pltpu.make_async_copy(gqbuf.at[me], gq_out.at[:, me], gq_recv.at[me]).start()
        for core, holder in enumerate(holders):
            copy = pltpu.make_async_remote_copy(
                gqbuf.at[holder], gq_out.at[:, me], gq_send.at[2 * step + core], gq_recv.at[me],
                device_id=(seq, holder), device_id_type=MESH,
            )
            copy.start()
            queries.append(copy)

    ds_chunk = score_gradients(0)
    key_total = None
    for step in range(chips):
        if step == 2:
            store_parts(0, *(
                jnp.dot(probs_half[rows_of, :], c2[...], preferred_element_type=jnp.float32)
                for rows_of in (pl.ds(0, tokens), pl.ds(2 * tokens, 2 * tokens))
            ))
            send_parts(0)
        later = score_gradients(step + 1) if step + 1 < chips else None
        query_gradients(step, ds_chunk)
        term = key_gradients(step, ds_chunk)
        key_total = term if key_total is None else key_total + term
        if later is None:
            key_total = key_total * scale
            store_parts(1, key_total[:tokens], key_total[2 * tokens:])
            own[1] = key_total[tokens:2 * tokens]
            send_parts(1)
        send_queries(step)
        ds_chunk = later

    own[0] = jnp.dot(probs_half[OWN * tokens:(OWN + 1) * tokens, :], c2[...], preferred_element_type=jnp.float32)
    outs = []
    for which, out in ((0, gv_out), (1, gk_out)):
        total = own[which]
        each_halo(1, lambda number: part_copy(which, number).wait_recv())
        for number in range(3):
            total = total + part_in[which, number].astype(jnp.float32)
        final[which] = total.astype(jnp.bfloat16)
        copy = pltpu.make_async_copy(final.at[which], out, out_sem.at[which])
        copy.start()
        outs.append(copy)
    for k in range(n_kvh):
        pltpu.make_async_copy(gqbuf.at[k], gq_out.at[:, k], gq_recv.at[k]).wait()
    for which in (0, 1):
        each_halo(1, lambda number: halo_copy(which, number).wait_send())
        each_halo(-1, lambda number: part_copy(which, number).wait_send())
    for copy in sends + queries:
        copy.wait_send()
    for copy in outs:
        copy.wait()


def finish(gq_in, gk_in, gv_in, gq_out, gk_out, gv_out, sem):
    copies = [
        pltpu.make_async_copy(source, target, sem.at[number])
        for number, (source, target) in enumerate(((gq_in, gq_out), (gk_in, gk_out), (gv_in, gv_out)))
    ]
    for copy in copies:
        copy.start()
    for copy in copies:
        copy.wait()


def solution(mesh):
    n_seq, n_kvh = mesh.shape["seq"], mesh.shape["kvh"]

    def step(queries, keys, values, output_gradient, doc_lengths, prefix_lengths):
        tokens, heads, size = queries.shape
        mine = output_gradient.shape[0]
        rows = tokens * heads
        bf16, f32, docs = jnp.bfloat16, jnp.float32, doc_lengths.shape[0]
        anywhere = pl.BlockSpec(memory_space=pl.ANY)
        dma = pltpu.SemaphoreType.DMA
        shapes = (
            jax.ShapeDtypeStruct((mine, n_kvh, heads, size), bf16),
            jax.ShapeDtypeStruct((tokens, size), bf16),
            jax.ShapeDtypeStruct((tokens, size), bf16),
        )
        results = pl.pallas_call(
            functools.partial(kernel, n_seq, n_kvh, size ** -0.5),
            out_shape=shapes,
            in_specs=[pl.BlockSpec(memory_space=pltpu.HBM)] * 6,
            out_specs=(anywhere,) * 3,
            scratch_shapes=[
                pltpu.VMEM((tokens, heads, size), bf16),
                pltpu.VMEM((TILES, tokens, size), bf16),
                pltpu.VMEM((TILES, tokens, size), bf16),
                pltpu.VMEM((n_kvh, mine, heads, size), bf16),
                pltpu.VMEM((1, docs), jnp.int32),
                pltpu.VMEM((1, docs), jnp.int32),
                pltpu.VMEM((rows, size), bf16),
                pltpu.VMEM((rows, size), bf16),
                pltpu.VMEM(((TILES - 1) * tokens, rows), f32),
                pltpu.VMEM((TILES * tokens, rows), bf16),
                pltpu.VMEM((n_kvh, mine, heads, size), bf16),
                pltpu.VMEM((2, 3, tokens, size), bf16),
                pltpu.VMEM((2, 3, tokens, size), bf16),
                pltpu.VMEM((2, tokens, size), f32),
                pltpu.VMEM((2, tokens, size), bf16),
                dma((5,)),
                dma((2, 3)),
                dma((2, 3)),
                dma((n_kvh,)),
                dma((n_kvh,)),
                dma((n_kvh,)),
                dma((n_kvh,)),
                dma((2, 3)),
                dma((2, 3)),
                dma((2,)),
                pltpu.SemaphoreType.REGULAR,
            ],
            compiler_params=pltpu.CompilerParams(collective_id=0, has_side_effects=True, vmem_limit_bytes=VMEM_LIMIT),
        )(*(pltpu.with_memory_space_constraint(x, pltpu.HBM) for x in (
            queries,
            keys.reshape(tokens, size),
            values.reshape(tokens, size),
            output_gradient.reshape(mine, n_kvh, heads, size),
            doc_lengths.reshape(1, docs),
            prefix_lengths.reshape(1, docs),
        )))
        gq, gk, gv = pl.pallas_call(
            finish,
            out_shape=shapes,
            in_specs=[anywhere] * 3,
            out_specs=(pl.BlockSpec(memory_space=pltpu.HBM),) * 3,
            scratch_shapes=[dma((3,))],
            compiler_params=pltpu.CompilerParams(vmem_limit_bytes=1 << 20),
        )(*results)
        return gq.reshape(mine, n_kvh * heads, size), gk.reshape(tokens, 1, size), gv.reshape(tokens, 1, size)

    return jax.shard_map(
        step,
        mesh=mesh,
        in_specs=(P("seq", "kvh", None),) * 3 + (P(("seq", "kvh"), None, None), P(), P()),
        out_specs=(P(("seq", "kvh"), None, None), P("seq", "kvh", None), P("seq", "kvh", None)),
        check_vma=False,
    )
```
